256 devices in a mesh: frame: 16 (over z_hi, y), space: 16 (over z_lo, x, core).
Axes of the slice: x: 4, y: 4, z: 8 (z_hi: 4, z_lo: 2; z = z_hi * 2 + z_lo), core: 2. Of those that a mesh axis runs over, the one named last changes fastest.
Arguments:
- hidden_in: bfloat16 [2, 16, 32, 64, 1152], P(None, 'frame', 'space'), may hold values from -6 to 6
- attn_cotangent: bfloat16 [2, 16, 32, 64, 1152], P(None, 'frame', 'space'), may hold values from -6 to 6
- w_qkv: bfloat16 [1152, 3456], P('space'), may hold values from -0.1875 to 0.1875
- modulation_table: bfloat16 [1000, 2, 1152], replicated, may hold values from -3 to 3
- snr_table: float32 [1000], replicated, may hold values from 0.1 to 1
- timestep: int32 [2], replicated, may hold values from 0 to 999
- weight_index: int32 [2], replicated, may hold values from 0 to 999
Outputs:
- grad_input: bfloat16 [2, 16, 32, 64, 1152], P(None, 'frame', 'space')
- grad_w_qkv: float32 [1152, 3456], P('space')
- grad_modulation: float32 [2, 2, 1152], replicated
The draws below stay inside these ranges and needn't reach their ends.
All inputs are finite; a program needn't handle non-finite values.
Results may differ from the reference program's by a relative error of at most 0.029.
Values may be sent and summed in bfloat16 or wider, within the bound.
A program may use at most 128 MiB of HBM per device.

```python
import math
import jax
import jax.numpy as jnp
from jax import lax

D = 1152
HEADS = 16
HEAD_DIM = 72
STEPS = 1000
CLIPS = 2
COLS = 64
FRAMES = 16
ROWS = 32


def level_of(rng, dims, cuts, low, high):
    level, own = 1.0, jax.random.fold_in(rng, 6)
    for position, shards_of in cuts:
        heights = jnp.exp(jax.random.uniform(jax.random.fold_in(own, position), (shards_of,), jnp.float32, low / len(cuts), high / len(cuts)))
        level = level * jnp.repeat(heights, dims[position] // shards_of).reshape([-1 if axis == position else 1 for axis in range(len(dims))])
    return level


def scatter_about(key, dims, spread, most, cuts=(), kind=jnp.bfloat16):
    array = jax.random.normal(key, dims, jnp.float32) * spread
    if len(cuts) > 0:
        array = level_of(key, dims, cuts, -0.22, 0.18) * array
    return jnp.clip(array, min=-most, max=most).astype(kind)


def setup_inputs(seed: int = 0) -> dict:
    key_of = jax.random.split(jax.random.key(seed), 8)
    hidden_in = scatter_about(key_of[0], (CLIPS, FRAMES, ROWS, COLS, D), 1.0, 6.0, ((1, 16), (2, 16)))
    attn_cotangent = scatter_about(key_of[1], (CLIPS, FRAMES, ROWS, COLS, D), 1.0, 6.0, ((1, 16), (2, 16)))
    w_qkv = scatter_about(key_of[2], (D, 3 * D), D ** -0.5, 0.1875, ((0, 16),))
    modulation_table = scatter_about(key_of[3], (STEPS, 2, D), 0.5, 3.0)
    snr_table = jnp.clip(jnp.exp(jax.random.uniform(key_of[4], (STEPS,), jnp.float32, math.log(0.1), math.log(1.0))), 0.1, 1.0)
    timestep = jax.random.randint(key_of[5], (CLIPS,), 0, STEPS).astype(jnp.int32)
    weight_index = jax.random.randint(key_of[6], (CLIPS,), 0, STEPS).astype(jnp.int32)
    return {"hidden_in": hidden_in, "attn_cotangent": attn_cotangent, "w_qkv": w_qkv, "modulation_table": modulation_table, "snr_table": snr_table, "timestep": timestep, "weight_index": weight_index}


def attend_back(queries, keys, values, upstream):
    factor = queries.shape[-1] ** (-0.5)
    queries = queries.astype(jnp.float32)
    keys = keys.astype(jnp.float32)
    values = values.astype(jnp.float32)
    upstream = upstream.astype(jnp.float32)
    highest = lax.Precision.HIGHEST
    scores = jnp.einsum('bfxhe,bgxhe->bxhfg', queries, keys, precision=highest) * factor
    expd = jnp.exp(scores)
    probs = expd / lax.optimization_barrier(jnp.sum(expd, axis=-1, keepdims=True))
    grad_probs = jnp.einsum('bfxhe,bgxhe->bxhfg', upstream, values, precision=highest)
    grad_values = jnp.einsum('bxhfg,bfxhe->bgxhe', probs, upstream, precision=highest)
    grad_scores = probs * (grad_probs - lax.optimization_barrier(jnp.sum(probs * grad_probs, axis=-1, keepdims=True)))
    grad_queries = jnp.einsum('bxhfg,bgxhe->bfxhe', grad_scores, keys, precision=highest) * factor
    grad_keys = jnp.einsum('bxhfg,bfxhe->bgxhe', grad_scores, queries, precision=highest) * factor
    return (grad_queries.astype(jnp.bfloat16), grad_keys.astype(jnp.bfloat16), grad_values.astype(jnp.bfloat16))

def reference(hidden_in, attn_cotangent, w_qkv, modulation_table, snr_table, timestep, weight_index):
    values_in = hidden_in.astype(jnp.float32)
    average = lax.optimization_barrier(jnp.mean(values_in, axis=-1, keepdims=True))
    centered = values_in - average
    variance = lax.optimization_barrier(jnp.mean(centered * centered, axis=-1, keepdims=True))
    inverse_std = lax.rsqrt(variance + 1e-06)
    normed = centered * inverse_std
    modulation = modulation_table[timestep].astype(jnp.float32)
    shift = modulation[:, 0][:, None, None, None, :]
    scale = modulation[:, 1][:, None, None, None, :]
    modulated = (normed * (1.0 + scale) + shift).astype(jnp.bfloat16)
    mod_rows = modulated.reshape(-1, D)
    projected = jnp.dot(mod_rows, w_qkv, preferred_element_type=jnp.float32).astype(jnp.bfloat16)
    projected = projected.reshape(CLIPS, FRAMES, ROWS * COLS, 3, HEADS, HEAD_DIM)
    loss_weight = snr_table[weight_index]
    upstream = (loss_weight[:, None, None, None, None] * attn_cotangent.astype(jnp.float32)).astype(jnp.bfloat16)
    upstream = upstream.reshape(CLIPS, FRAMES, ROWS * COLS, HEADS, HEAD_DIM)
    grad_queries, grad_keys, grad_values = attend_back(projected[:, :, :, 0], projected[:, :, :, 1], projected[:, :, :, 2], upstream)
    grad_projected = jnp.stack([grad_queries, grad_keys, grad_values], axis=3).reshape(-1, 3 * D)
    grad_scale_factor = float(CLIPS * FRAMES * ROWS * COLS) ** (-0.5)
    grad_weight = jnp.dot(mod_rows.T, grad_projected, preferred_element_type=jnp.float32) * grad_scale_factor
    grad_hidden = jnp.dot(grad_projected, w_qkv.T, preferred_element_type=jnp.float32).reshape(values_in.shape)
    shift_sums = lax.optimization_barrier(jnp.sum(grad_hidden, axis=(1, 2, 3)))
    scale_sums = lax.optimization_barrier(jnp.sum(grad_hidden * normed, axis=(1, 2, 3)))
    grad_modulation = jnp.stack([shift_sums, scale_sums], axis=1) * grad_scale_factor
    grad_normed = grad_hidden * (1.0 + scale)
    grad_input = (grad_normed - lax.optimization_barrier(jnp.mean(grad_normed, axis=-1, keepdims=True)) - normed * lax.optimization_barrier(jnp.mean(grad_normed * normed, axis=-1, keepdims=True))) * inverse_std
    return (grad_input.astype(jnp.bfloat16), grad_weight, grad_modulation)
```

```python
import jax
import jax.numpy as jnp
from jax import lax
from jax.sharding import PartitionSpec as P

HEADS = 16
HEAD_DIM = 72


def attend_back(queries, keys, values, upstream):
    factor = queries.shape[-1] ** (-0.5)
    queries = queries.astype(jnp.float32)
    keys = keys.astype(jnp.float32)
    values = values.astype(jnp.float32)
    upstream = upstream.astype(jnp.float32)
    highest = lax.Precision.HIGHEST
    scores = jnp.einsum("bfxhe,bgxhe->bxhfg", queries, keys, precision=highest) * factor
    expd = jnp.exp(scores)
    probs = expd / jnp.sum(expd, axis=-1, keepdims=True)
    grad_probs = jnp.einsum("bfxhe,bgxhe->bxhfg", upstream, values, precision=highest)
    grad_values = jnp.einsum("bxhfg,bfxhe->bgxhe", probs, upstream, precision=highest)
    grad_scores = probs * (grad_probs - jnp.sum(probs * grad_probs, axis=-1, keepdims=True))
    grad_queries = jnp.einsum("bxhfg,bgxhe->bfxhe", grad_scores, keys, precision=highest) * factor
    grad_keys = jnp.einsum("bxhfg,bfxhe->bgxhe", grad_scores, queries, precision=highest) * factor
    return (
        grad_queries.astype(jnp.bfloat16),
        grad_keys.astype(jnp.bfloat16),
        grad_values.astype(jnp.bfloat16),
    )


def per_device(
    hidden_in, attn_cotangent, w_qkv, modulation_table, snr_table, timestep, weight_index
):
    clip_count, frame_dev, row_dev, col_count, model_width = hidden_in.shape
    frame_n = lax.axis_size("frame")
    space_n = lax.axis_size("space")
    positions = row_dev * col_count
    w_full = lax.all_gather(w_qkv, "space", axis=0, tiled=True)
    both = jnp.stack(
        [
            hidden_in.reshape(clip_count, frame_dev, positions, model_width),
            attn_cotangent.reshape(clip_count, frame_dev, positions, model_width),
        ],
        axis=3,
    )
    both = lax.all_to_all(both, "frame", split_axis=2, concat_axis=1, tiled=True)
    frames = both.shape[1]
    across = both.shape[2]
    values_in = both[:, :, :, 0].astype(jnp.float32)
    average = jnp.mean(values_in, axis=-1, keepdims=True)
    centered = values_in - average
    variance = jnp.mean(centered * centered, axis=-1, keepdims=True)
    inverse_std = lax.rsqrt(variance + 1e-06)
    normed = centered * inverse_std
    modulation = modulation_table[timestep].astype(jnp.float32)
    shift = modulation[:, 0][:, None, None, :]
    scale = modulation[:, 1][:, None, None, :]
    modulated = (normed * (1.0 + scale) + shift).astype(jnp.bfloat16)
    mod_rows = modulated.reshape(-1, model_width)
    projected = jnp.dot(mod_rows, w_full, preferred_element_type=jnp.float32).astype(jnp.bfloat16)
    pieces = projected.reshape(clip_count, frames, across, 3, HEADS, HEAD_DIM)
    loss_weight = snr_table[weight_index]
    upstream = (
        loss_weight[:, None, None, None] * both[:, :, :, 1].astype(jnp.float32)
    ).astype(jnp.bfloat16)
    upstream = upstream.reshape(clip_count, frames, across, HEADS, HEAD_DIM)
    head_grads = attend_back(pieces[:, :, :, 0], pieces[:, :, :, 1], pieces[:, :, :, 2], upstream)
    grad_rows = jnp.stack(head_grads, axis=3).reshape(-1, 3 * model_width)
    grad_scale_factor = float(mod_rows.shape[0] * frame_n * space_n) ** (-0.5)
    term = lax.dot_general(
        mod_rows, grad_rows, (((0,), (0,)), ((), ())), preferred_element_type=jnp.float32
    ).astype(jnp.bfloat16)
    col_blk = 3 * model_width // frame_n
    share = lax.psum_scatter(term, "space", scatter_dimension=0, tiled=True)
    share = share.reshape(share.shape[0], frame_n, col_blk)
    share = lax.psum_scatter(share, "frame", scatter_dimension=1, tiled=True)
    grad_weight = lax.all_gather(share, "frame", axis=1, tiled=True)
    grad_weight = grad_weight.reshape(share.shape[0], 3 * model_width)
    grad_weight = grad_weight.astype(jnp.float32) * grad_scale_factor
    grad_hidden = lax.dot_general(
        grad_rows, w_full, (((1,), (1,)), ((), ())), preferred_element_type=jnp.float32
    )
    grad_hidden = grad_hidden.reshape(values_in.shape)
    local_sums = jnp.stack(
        [jnp.sum(grad_hidden, axis=(1, 2)), jnp.sum(grad_hidden * normed, axis=(1, 2))],
        axis=1,
    )
    grad_modulation = lax.psum(local_sums, ("frame", "space")) * grad_scale_factor
    grad_normed = grad_hidden * (1.0 + scale)
    grad_input = (
        grad_normed
        - jnp.mean(grad_normed, axis=-1, keepdims=True)
        - normed * jnp.mean(grad_normed * normed, axis=-1, keepdims=True)
    ) * inverse_std
    grad_input = grad_input.astype(jnp.bfloat16)
    grad_input = lax.all_to_all(grad_input, "frame", split_axis=1, concat_axis=2, tiled=True)
    grad_input = grad_input.reshape(clip_count, frame_dev, row_dev, col_count, model_width)
    return (grad_input, grad_weight, grad_modulation)


def solution(mesh):
    in_specs = (
        P(None, "frame", "space", None, None),
        P(None, "frame", "space", None, None),
        P("space", None),
        P(),
        P(),
        P(),
        P(),
    )
    out_specs = (P(None, "frame", "space", None, None), P("space", None), P())
    return jax.shard_map(
        per_device, mesh=mesh, in_specs=in_specs, out_specs=out_specs, check_vma=False
    )
```

```python
import functools

import jax
import jax.numpy as jnp
from jax import lax
from jax.experimental import pallas as pl
from jax.experimental.pallas import tpu as pltpu
from jax.sharding import PartitionSpec as P

MESH = pl.DeviceIdType.MESH

HEADS = 16
HEAD_DIM = 72


def attend_back(queries, keys, values, upstream):
    factor = queries.shape[-1] ** (-0.5)
    queries = queries.astype(jnp.float32)
    keys = keys.astype(jnp.float32)
    values = values.astype(jnp.float32)
    upstream = upstream.astype(jnp.float32)
    highest = lax.Precision.HIGHEST
    scores = jnp.einsum("bfxhe,bgxhe->bxhfg", queries, keys, precision=highest) * factor
    expd = jnp.exp(scores)
    probs = expd / jnp.sum(expd, axis=-1, keepdims=True)
    grad_probs = jnp.einsum("bfxhe,bgxhe->bxhfg", upstream, values, precision=highest)
    grad_values = jnp.einsum("bxhfg,bfxhe->bgxhe", probs, upstream, precision=highest)
    grad_scores = probs * (grad_probs - jnp.sum(probs * grad_probs, axis=-1, keepdims=True))
    grad_queries = jnp.einsum("bxhfg,bgxhe->bfxhe", grad_scores, keys, precision=highest) * factor
    grad_keys = jnp.einsum("bxhfg,bfxhe->bgxhe", grad_scores, queries, precision=highest) * factor
    return (
        grad_queries.astype(jnp.bfloat16),
        grad_keys.astype(jnp.bfloat16),
        grad_values.astype(jnp.bfloat16),
    )


def reduce_kernel(
    nf, ns, chunks_ref, sums_ref, gw_ref, gm_ref,
    recv1, msum1, redbuf, mbuf, recv2, msum2, s1c, r1c, s1m, r1m, s2c, r2c, s2m, r2m,
):
    me_f = lax.axis_index("frame")
    me_s = lax.axis_index("space")
    barrier = pltpu.get_barrier_semaphore()
    for k in range(1, nf):
        pl.semaphore_signal(
            barrier, inc=1, device_id=(lax.rem(me_f + k, nf), me_s), device_id_type=MESH
        )
    for k in range(1, ns):
        pl.semaphore_signal(
            barrier, inc=1, device_id=(me_f, lax.rem(me_s + k, ns)), device_id_type=MESH
        )
    pl.semaphore_wait(barrier, (nf - 1) + (ns - 1))

    sends = []
    for k in range(1, nf):
        t = lax.rem(me_f + k, nf)
        c = pltpu.make_async_remote_copy(
            src_ref=chunks_ref.at[t], dst_ref=recv1.at[me_f], send_sem=s1c.at[k],
            recv_sem=r1c.at[me_f], device_id=(t, me_s), device_id_type=MESH,
        )
        c.start()
        m = pltpu.make_async_remote_copy(
            src_ref=sums_ref, dst_ref=msum1.at[me_f], send_sem=s1m.at[k],
            recv_sem=r1m.at[me_f], device_id=(t, me_s), device_id_type=MESH,
        )
        m.start()
        sends += [c, m]
    recv1[me_f] = chunks_ref[me_f]
    msum1[me_f] = sums_ref[...]
    for k in range(1, nf):
        src = lax.rem(me_f + nf - k, nf)
        pltpu.make_async_remote_copy(
            src_ref=chunks_ref.at[0], dst_ref=recv1.at[src], send_sem=s1c.at[k],
            recv_sem=r1c.at[src], device_id=(src, me_s), device_id_type=MESH,
        ).wait_recv()
        pltpu.make_async_remote_copy(
            src_ref=sums_ref, dst_ref=msum1.at[src], send_sem=s1m.at[k],
            recv_sem=r1m.at[src], device_id=(src, me_s), device_id_type=MESH,
        ).wait_recv()
    for c in sends:
        c.wait_send()
    acc = recv1[0].astype(jnp.float32)
    macc = msum1[0]
    for j in range(1, nf):
        acc = acc + recv1[j].astype(jnp.float32)
        macc = macc + msum1[j]
    redbuf[...] = acc
    mbuf[...] = macc
    recv2[me_f] = acc
    msum2[me_s] = macc

    sends = []
    for k in range(1, nf):
        t = lax.rem(me_f + k, nf)
        c = pltpu.make_async_remote_copy(
            src_ref=redbuf, dst_ref=recv2.at[me_f], send_sem=s2c.at[k],
            recv_sem=r2c.at[me_f], device_id=(t, me_s), device_id_type=MESH,
        )
        c.start()
        sends.append(c)
    for k in range(1, ns):
        t = lax.rem(me_s + k, ns)
        m = pltpu.make_async_remote_copy(
            src_ref=mbuf, dst_ref=msum2.at[me_s], send_sem=s2m.at[k],
            recv_sem=r2m.at[me_s], device_id=(me_f, t), device_id_type=MESH,
        )
        m.start()
        sends.append(m)
    for k in range(1, nf):
        src = lax.rem(me_f + nf - k, nf)
        pltpu.make_async_remote_copy(
            src_ref=redbuf, dst_ref=recv2.at[src], send_sem=s2c.at[k],
            recv_sem=r2c.at[src], device_id=(src, me_s), device_id_type=MESH,
        ).wait_recv()
    for k in range(1, ns):
        src = lax.rem(me_s + ns - k, ns)
        pltpu.make_async_remote_copy(
            src_ref=mbuf, dst_ref=msum2.at[src], send_sem=s2m.at[k],
            recv_sem=r2m.at[src], device_id=(me_f, src), device_id_type=MESH,
        ).wait_recv()
    for c in sends:
        c.wait_send()
    gw_ref[...] = recv2[...]
    total = msum2[0]
    for j in range(1, ns):
        total = total + msum2[j]
    gm_ref[...] = total


def reduce_frame(chunks, sums, nf, ns):
    count, rows, cols = chunks.shape
    vmem = pl.BlockSpec(memory_space=pltpu.VMEM)
    return pl.pallas_call(
        functools.partial(reduce_kernel, nf, ns),
        out_shape=(
            jax.ShapeDtypeStruct((count, rows, cols), jnp.float32),
            jax.ShapeDtypeStruct(sums.shape, jnp.float32),
        ),
        in_specs=[vmem, vmem],
        out_specs=(vmem, vmem),
        scratch_shapes=[
            pltpu.VMEM((nf, rows, cols), chunks.dtype),
            pltpu.VMEM((nf,) + sums.shape, jnp.float32),
            pltpu.VMEM((rows, cols), jnp.float32),
            pltpu.VMEM(sums.shape, jnp.float32),
            pltpu.VMEM((nf, rows, cols), jnp.float32),
            pltpu.VMEM((ns,) + sums.shape, jnp.float32),
        ]
        + [pltpu.SemaphoreType.DMA((max(nf, ns),))] * 8,
        compiler_params=pltpu.CompilerParams(collective_id=0, has_side_effects=True),
    )(chunks, sums)


def per_device(
    hidden_in, attn_cotangent, w_qkv, modulation_table, snr_table, timestep, weight_index
):
    clip_count, frame_dev, row_dev, col_count, model_width = hidden_in.shape
    frame_n = lax.axis_size("frame")
    space_n = lax.axis_size("space")
    positions = row_dev * col_count
    w_full = lax.all_gather(w_qkv, "space", axis=0, tiled=True)
    both = jnp.stack(
        [
            hidden_in.reshape(clip_count, frame_dev, positions, model_width),
            attn_cotangent.reshape(clip_count, frame_dev, positions, model_width),
        ],
        axis=3,
    )
    both = lax.all_to_all(both, "frame", split_axis=2, concat_axis=1, tiled=True)
    frames = both.shape[1]
    across = both.shape[2]
    values_in = both[:, :, :, 0].astype(jnp.float32)
    average = jnp.mean(values_in, axis=-1, keepdims=True)
    centered = values_in - average
    variance = jnp.mean(centered * centered, axis=-1, keepdims=True)
    inverse_std = lax.rsqrt(variance + 1e-06)
    normed = centered * inverse_std
    modulation = modulation_table[timestep].astype(jnp.float32)
    shift = modulation[:, 0][:, None, None, :]
    scale = modulation[:, 1][:, None, None, :]
    modulated = (normed * (1.0 + scale) + shift).astype(jnp.bfloat16)
    mod_rows = modulated.reshape(-1, model_width)
    projected = jnp.dot(mod_rows, w_full, preferred_element_type=jnp.float32).astype(jnp.bfloat16)
    pieces = projected.reshape(clip_count, frames, across, 3, HEADS, HEAD_DIM)
    loss_weight = snr_table[weight_index]
    upstream = (
        loss_weight[:, None, None, None] * both[:, :, :, 1].astype(jnp.float32)
    ).astype(jnp.bfloat16)
    upstream = upstream.reshape(clip_count, frames, across, HEADS, HEAD_DIM)
    head_grads = attend_back(pieces[:, :, :, 0], pieces[:, :, :, 1], pieces[:, :, :, 2], upstream)
    grad_rows = jnp.stack(head_grads, axis=3).reshape(-1, 3 * model_width)
    grad_scale_factor = float(mod_rows.shape[0] * frame_n * space_n) ** (-0.5)
    term = lax.dot_general(
        mod_rows, grad_rows, (((0,), (0,)), ((), ())), preferred_element_type=jnp.float32
    ).astype(jnp.bfloat16)
    col_blk = 3 * model_width // frame_n
    share = lax.psum_scatter(term, "space", scatter_dimension=0, tiled=True)
    row_blk = share.shape[0]
    share = share.reshape(row_blk, frame_n, col_blk).transpose(1, 0, 2)
    grad_hidden = lax.dot_general(
        grad_rows, w_full, (((1,), (1,)), ((), ())), preferred_element_type=jnp.float32
    )
    grad_hidden = grad_hidden.reshape(values_in.shape)
    local_sums = jnp.stack(
        [jnp.sum(grad_hidden, axis=(1, 2)), jnp.sum(grad_hidden * normed, axis=(1, 2))],
        axis=1,
    )
    local_sums = local_sums.reshape(-1, model_width)
    gw, gm = reduce_frame(share, local_sums, frame_n, space_n)
    grad_weight = gw.transpose(1, 0, 2).reshape(row_blk, 3 * model_width) * grad_scale_factor
    grad_modulation = gm.reshape(clip_count, 2, model_width) * grad_scale_factor
    grad_normed = grad_hidden * (1.0 + scale)
    grad_input = (
        grad_normed
        - jnp.mean(grad_normed, axis=-1, keepdims=True)
        - normed * jnp.mean(grad_normed * normed, axis=-1, keepdims=True)
    ) * inverse_std
    grad_input = grad_input.astype(jnp.bfloat16)
    grad_input = lax.all_to_all(grad_input, "frame", split_axis=1, concat_axis=2, tiled=True)
    grad_input = grad_input.reshape(clip_count, frame_dev, row_dev, col_count, model_width)
    return (grad_input, grad_weight, grad_modulation)


def solution(mesh):
    in_specs = (
        P(None, "frame", "space", None, None),
        P(None, "frame", "space", None, None),
        P("space", None),
        P(),
        P(),
        P(),
        P(),
    )
    out_specs = (P(None, "frame", "space", None, None), P("space", None), P())
    return jax.shard_map(
        per_device, mesh=mesh, in_specs=in_specs, out_specs=out_specs, check_vma=False
    )
```

```python
import functools

import jax
import jax.numpy as jnp
from jax import lax
from jax.experimental import pallas as pl
from jax.experimental.pallas import tpu as pltpu
from jax.sharding import PartitionSpec as P

MESH = pl.DeviceIdType.MESH

HEADS = 16
HEAD_DIM = 72


def attend_back(queries, keys, values, upstream):
    factor = queries.shape[-1] ** (-0.5)
    queries = queries.astype(jnp.float32)
    keys = keys.astype(jnp.float32)
    values = values.astype(jnp.float32)
    upstream = upstream.astype(jnp.float32)
    highest = lax.Precision.HIGHEST
    scores = jnp.einsum("bfxhe,bgxhe->bxhfg", queries, keys, precision=highest) * factor
    expd = jnp.exp(scores)
    probs = expd / jnp.sum(expd, axis=-1, keepdims=True)
    grad_probs = jnp.einsum("bfxhe,bgxhe->bxhfg", upstream, values, precision=highest)
    grad_values = jnp.einsum("bxhfg,bfxhe->bgxhe", probs, upstream, precision=highest)
    grad_scores = probs * (grad_probs - jnp.sum(probs * grad_probs, axis=-1, keepdims=True))
    grad_queries = jnp.einsum("bxhfg,bgxhe->bfxhe", grad_scores, keys, precision=highest) * factor
    grad_keys = jnp.einsum("bxhfg,bfxhe->bgxhe", grad_scores, queries, precision=highest) * factor
    return (
        grad_queries.astype(jnp.bfloat16),
        grad_keys.astype(jnp.bfloat16),
        grad_values.astype(jnp.bfloat16),
    )


def reduce_kernel(
    nf, sub, chunks_ref, sums_ref, gw_ref, gm_ref,
    recv1, msum1, redbuf, mbuf, recv2, msum2, s1c, r1c, s1m, r1m, s2c, r2c, s2m, r2m,
):
    nz, nx, nc = sub
    ns = nz * nx * nc
    me_f = lax.axis_index("frame")
    me_s = (lax.axis_index("sz") * nx + lax.axis_index("sx")) * nc + lax.axis_index("sc")

    def dev(f, s):
        return (f, s // (nx * nc), lax.rem(s // nc, nx), lax.rem(s, nc))
    barrier = pltpu.get_barrier_semaphore()
    for k in range(1, nf):
        pl.semaphore_signal(
            barrier, inc=1, device_id=dev(lax.rem(me_f + k, nf), me_s), device_id_type=MESH
        )
    for k in range(1, ns):
        pl.semaphore_signal(
            barrier, inc=1, device_id=dev(me_f, lax.rem(me_s + k, ns)), device_id_type=MESH
        )
    pl.semaphore_wait(barrier, (nf - 1) + (ns - 1))

    sends = []
    for k in range(1, nf):
        t = lax.rem(me_f + k, nf)
        c = pltpu.make_async_remote_copy(
            src_ref=chunks_ref.at[t], dst_ref=recv1.at[me_f], send_sem=s1c.at[k],
            recv_sem=r1c.at[me_f], device_id=dev(t, me_s), device_id_type=MESH,
        )
        c.start()
        m = pltpu.make_async_remote_copy(
            src_ref=sums_ref, dst_ref=msum1.at[me_f], send_sem=s1m.at[k],
            recv_sem=r1m.at[me_f], device_id=dev(t, me_s), device_id_type=MESH,
        )
        m.start()
        sends += [c, m]
    recv1[me_f] = chunks_ref[me_f]
    msum1[me_f] = sums_ref[...]
    for k in range(1, nf):
        src = lax.rem(me_f + nf - k, nf)
        pltpu.make_async_remote_copy(
            src_ref=chunks_ref.at[0], dst_ref=recv1.at[src], send_sem=s1c.at[k],
            recv_sem=r1c.at[src], device_id=dev(src, me_s), device_id_type=MESH,
        ).wait_recv()
        pltpu.make_async_remote_copy(
            src_ref=sums_ref, dst_ref=msum1.at[src], send_sem=s1m.at[k],
            recv_sem=r1m.at[src], device_id=dev(src, me_s), device_id_type=MESH,
        ).wait_recv()
    for c in sends:
        c.wait_send()
    acc = recv1[0].astype(jnp.float32)
    macc = msum1[0]
    for j in range(1, nf):
        acc = acc + recv1[j].astype(jnp.float32)
        macc = macc + msum1[j]
    redbuf[...] = acc
    mbuf[...] = macc
    recv2[me_f] = acc
    msum2[me_s] = macc

    sends = []
    for k in range(1, nf):
        t = lax.rem(me_f + k, nf)
        c = pltpu.make_async_remote_copy(
            src_ref=redbuf, dst_ref=recv2.at[me_f], send_sem=s2c.at[k],
            recv_sem=r2c.at[me_f], device_id=dev(t, me_s), device_id_type=MESH,
        )
        c.start()
        sends.append(c)
    for k in range(1, ns):
        t = lax.rem(me_s + k, ns)
        m = pltpu.make_async_remote_copy(
            src_ref=mbuf, dst_ref=msum2.at[me_s], send_sem=s2m.at[k],
            recv_sem=r2m.at[me_s], device_id=dev(me_f, t), device_id_type=MESH,
        )
        m.start()
        sends.append(m)
    for k in range(1, nf):
        src = lax.rem(me_f + nf - k, nf)
        pltpu.make_async_remote_copy(
            src_ref=redbuf, dst_ref=recv2.at[src], send_sem=s2c.at[k],
            recv_sem=r2c.at[src], device_id=dev(src, me_s), device_id_type=MESH,
        ).wait_recv()
    for k in range(1, ns):
        src = lax.rem(me_s + ns - k, ns)
        pltpu.make_async_remote_copy(
            src_ref=mbuf, dst_ref=msum2.at[src], send_sem=s2m.at[k],
            recv_sem=r2m.at[src], device_id=dev(me_f, src), device_id_type=MESH,
        ).wait_recv()
    for c in sends:
        c.wait_send()
    gw_ref[...] = recv2[...]
    total = msum2[0]
    for j in range(1, ns):
        total = total + msum2[j]
    gm_ref[...] = total


def reduce_frame(chunks, sums, nf, sub):
    count, rows, cols = chunks.shape
    vmem = pl.BlockSpec(memory_space=pltpu.VMEM)
    return pl.pallas_call(
        functools.partial(reduce_kernel, nf, sub),
        out_shape=(
            jax.ShapeDtypeStruct((count, rows, cols), jnp.float32),
            jax.ShapeDtypeStruct(sums.shape, jnp.float32),
        ),
        in_specs=[vmem, vmem],
        out_specs=(vmem, vmem),
        scratch_shapes=[
            pltpu.VMEM((nf, rows, cols), chunks.dtype),
            pltpu.VMEM((nf,) + sums.shape, jnp.float32),
            pltpu.VMEM((rows, cols), jnp.float32),
            pltpu.VMEM(sums.shape, jnp.float32),
            pltpu.VMEM((nf, rows, cols), jnp.float32),
            pltpu.VMEM((sub[0] * sub[1] * sub[2],) + sums.shape, jnp.float32),
        ]
        + [pltpu.SemaphoreType.DMA((max(nf, sub[0] * sub[1] * sub[2]),))] * 8,
        compiler_params=pltpu.CompilerParams(collective_id=0, has_side_effects=True),
    )(chunks, sums)


def per_device(
    hidden_in, attn_cotangent, w_qkv, modulation_table, snr_table, timestep, weight_index
):
    clip_count, frame_dev, row_dev, col_count, model_width = hidden_in.shape
    frame_n = lax.axis_size("frame")
    sub = (lax.axis_size("sz"), lax.axis_size("sx"), lax.axis_size("sc"))
    space_n = sub[0] * sub[1] * sub[2]
    positions = row_dev * col_count
    w_full = lax.all_gather(w_qkv, "sz", axis=0)
    w_full = lax.all_gather(w_full, "sx", axis=0)
    w_full = lax.all_gather(w_full, "sc", axis=0)
    w_full = w_full.reshape(-1, w_qkv.shape[1])
    both = jnp.stack(
        [
            hidden_in.reshape(clip_count, frame_dev, positions, model_width),
            attn_cotangent.reshape(clip_count, frame_dev, positions, model_width),
        ],
        axis=3,
    )
    both = lax.all_to_all(both, "frame", split_axis=2, concat_axis=1, tiled=True)
    frames = both.shape[1]
    across = both.shape[2]
    values_in = both[:, :, :, 0].astype(jnp.float32)
    average = jnp.mean(values_in, axis=-1, keepdims=True)
    centered = values_in - average
    variance = jnp.mean(centered * centered, axis=-1, keepdims=True)
    inverse_std = lax.rsqrt(variance + 1e-06)
    normed = centered * inverse_std
    modulation = modulation_table[timestep].astype(jnp.float32)
    shift = modulation[:, 0][:, None, None, :]
    scale = modulation[:, 1][:, None, None, :]
    modulated = (normed * (1.0 + scale) + shift).astype(jnp.bfloat16)
    row_blk = model_width // space_n
    mod_rows = modulated.reshape((-1,) + sub + (row_blk,)).transpose(0, 3, 2, 1, 4)
    mod_rows = mod_rows.reshape(-1, model_width)
    projected = jnp.dot(mod_rows, w_full, preferred_element_type=jnp.float32).astype(jnp.bfloat16)
    pieces = projected.reshape(clip_count, frames, across, 3, HEADS, HEAD_DIM)
    loss_weight = snr_table[weight_index]
    upstream = (
        loss_weight[:, None, None, None] * both[:, :, :, 1].astype(jnp.float32)
    ).astype(jnp.bfloat16)
    upstream = upstream.reshape(clip_count, frames, across, HEADS, HEAD_DIM)
    head_grads = attend_back(pieces[:, :, :, 0], pieces[:, :, :, 1], pieces[:, :, :, 2], upstream)
    grad_rows = jnp.stack(head_grads, axis=3).reshape(-1, 3 * model_width)
    grad_scale_factor = float(mod_rows.shape[0] * frame_n * space_n) ** (-0.5)
    term = lax.dot_general(
        mod_rows, grad_rows, (((0,), (0,)), ((), ())), preferred_element_type=jnp.float32
    ).astype(jnp.bfloat16)
    col_blk = 3 * model_width // frame_n
    share = term.reshape(sub[2], -1, 3 * model_width)
    share = lax.psum_scatter(share, "sc", scatter_dimension=0, tiled=True)
    share = share.reshape(sub[1], -1, 3 * model_width)
    share = lax.psum_scatter(share, "sx", scatter_dimension=0, tiled=True)
    share = share.reshape(sub[0], -1, 3 * model_width)
    share = lax.psum_scatter(share, "sz", scatter_dimension=0, tiled=True)
    share = share.reshape(row_blk, frame_n, col_blk).transpose(1, 0, 2)
    grad_hidden = lax.dot_general(
        grad_rows, w_full, (((1,), (1,)), ((), ())), preferred_element_type=jnp.float32
    )
    grad_hidden = grad_hidden.reshape((-1,) + sub[::-1] + (row_blk,)).transpose(0, 3, 2, 1, 4)
    grad_hidden = grad_hidden.reshape(values_in.shape)
    local_sums = jnp.stack(
        [jnp.sum(grad_hidden, axis=(1, 2)), jnp.sum(grad_hidden * normed, axis=(1, 2))],
        axis=1,
    )
    local_sums = local_sums.reshape(-1, model_width)
    gw, gm = reduce_frame(share, local_sums, frame_n, sub)
    grad_weight = gw.transpose(1, 0, 2).reshape(row_blk, 3 * model_width) * grad_scale_factor
    grad_modulation = gm.reshape(clip_count, 2, model_width) * grad_scale_factor
    grad_normed = grad_hidden * (1.0 + scale)
    grad_input = (
        grad_normed
        - jnp.mean(grad_normed, axis=-1, keepdims=True)
        - normed * jnp.mean(grad_normed * normed, axis=-1, keepdims=True)
    ) * inverse_std
    grad_input = grad_input.astype(jnp.bfloat16)
    grad_input = lax.all_to_all(grad_input, "frame", split_axis=1, concat_axis=2, tiled=True)
    grad_input = grad_input.reshape(clip_count, frame_dev, row_dev, col_count, model_width)
    return (grad_input, grad_weight, grad_modulation)


def solution(mesh):
    space_sub = (2, 4, 2)
    devices = mesh.devices.reshape((mesh.shape["frame"],) + space_sub)
    fine = jax.sharding.Mesh(devices, ("frame", "sz", "sx", "sc"))
    space = ("sz", "sx", "sc")
    in_specs = (
        P(None, "frame", space, None, None),
        P(None, "frame", space, None, None),
        P(space, None),
        P(),
        P(),
        P(),
        P(),
    )
    out_specs = (P(None, "frame", space, None, None), P(space, None), P())
    return jax.shard_map(
        per_device, mesh=fine, in_specs=in_specs, out_specs=out_specs, check_vma=False
    )
```

```python
import functools

import jax
import jax.numpy as jnp
from jax import lax
from jax.experimental import pallas as pl
from jax.experimental.pallas import tpu as pltpu
from jax.sharding import PartitionSpec as P

MESH = pl.DeviceIdType.MESH

HEADS = 16
HEAD_DIM = 72


def attend_back(queries, keys, values, upstream):
    factor = queries.shape[-1] ** (-0.5)
    queries = queries.astype(jnp.float32)
    keys = keys.astype(jnp.float32)
    values = values.astype(jnp.float32)
    upstream = upstream.astype(jnp.float32)
    highest = lax.Precision.HIGHEST
    scores = jnp.einsum("bfxhe,bgxhe->bxhfg", queries, keys, precision=highest) * factor
    expd = jnp.exp(scores)
    probs = expd / jnp.sum(expd, axis=-1, keepdims=True)
    grad_probs = jnp.einsum("bfxhe,bgxhe->bxhfg", upstream, values, precision=highest)
    grad_values = jnp.einsum("bxhfg,bfxhe->bgxhe", probs, upstream, precision=highest)
    grad_scores = probs * (grad_probs - jnp.sum(probs * grad_probs, axis=-1, keepdims=True))
    grad_queries = jnp.einsum("bxhfg,bgxhe->bfxhe", grad_scores, keys, precision=highest) * factor
    grad_keys = jnp.einsum("bxhfg,bfxhe->bgxhe", grad_scores, queries, precision=highest) * factor
    return (
        grad_queries.astype(jnp.bfloat16),
        grad_keys.astype(jnp.bfloat16),
        grad_values.astype(jnp.bfloat16),
    )


def barrier_with(peers):
    barrier = pltpu.get_barrier_semaphore()
    for p in peers:
        pl.semaphore_signal(barrier, inc=1, device_id=p, device_id_type=MESH)
    pl.semaphore_wait(barrier, len(peers))


def exchange(src_ref, dst, peer_of, index_of, count, send_sem, recv_sem):
    sends = []
    for k in range(1, count):
        t = lax.rem(index_of + k, count)
        c = pltpu.make_async_remote_copy(
            src_ref=src_ref(t), dst_ref=dst.at[index_of], send_sem=send_sem.at[k],
            recv_sem=recv_sem.at[index_of], device_id=peer_of(t), device_id_type=MESH,
        )
        c.start()
        sends.append(c)
    return sends


def wait_all(src_ref, dst, peer_of, index_of, count, send_sem, recv_sem, sends):
    for k in range(1, count):
        src = lax.rem(index_of + count - k, count)
        pltpu.make_async_remote_copy(
            src_ref=src_ref(0), dst_ref=dst.at[src], send_sem=send_sem.at[k],
            recv_sem=recv_sem.at[src], device_id=peer_of(src), device_id_type=MESH,
        ).wait_recv()
    for c in sends:
        c.wait_send()


def weight_kernel(nf, chunks_ref, gw_ref, recv1, redbuf, recv2, s1, r1, s2, r2):
    me_f = lax.axis_index("frame")
    me_s = lax.axis_index("space")
    peer = lambda t: (t, me_s)
    barrier_with([peer(lax.rem(me_f + k, nf)) for k in range(1, nf)])
    first = lambda t: chunks_ref.at[t]
    sends = exchange(first, recv1, peer, me_f, nf, s1, r1)
    recv1[me_f] = chunks_ref[me_f]
    wait_all(first, recv1, peer, me_f, nf, s1, r1, sends)
    acc = recv1[0].astype(jnp.float32)
    for j in range(1, nf):
        acc = acc + recv1[j].astype(jnp.float32)
    acc = acc.astype(redbuf.dtype)
    redbuf[...] = acc
    recv2[me_f] = acc
    second = lambda t: redbuf
    sends = exchange(second, recv2, peer, me_f, nf, s2, r2)
    wait_all(second, recv2, peer, me_f, nf, s2, r2, sends)
    gw_ref[...] = recv2[...]


def sums_kernel(nf, ns, sums_ref, gm_ref, msum1, mbuf, msum2, s1, r1, s2, r2):
    me_f = lax.axis_index("frame")
    me_s = lax.axis_index("space")
    fpeer = lambda t: (t, me_s)
    speer = lambda t: (me_f, t)
    barrier_with(
        [fpeer(lax.rem(me_f + k, nf)) for k in range(1, nf)]
        + [speer(lax.rem(me_s + k, ns)) for k in range(1, ns)]
    )
    first = lambda t: sums_ref
    sends = exchange(first, msum1, fpeer, me_f, nf, s1, r1)
    msum1[me_f] = sums_ref[...]
    wait_all(first, msum1, fpeer, me_f, nf, s1, r1, sends)
    macc = msum1[0]
    for j in range(1, nf):
        macc = macc + msum1[j]
    mbuf[...] = macc
    msum2[me_s] = macc
    second = lambda t: mbuf
    sends = exchange(second, msum2, speer, me_s, ns, s2, r2)
    wait_all(second, msum2, speer, me_s, ns, s2, r2, sends)
    total = msum2[0]
    for j in range(1, ns):
        total = total + msum2[j]
    gm_ref[...] = total


def reduce_weight(chunks, nf):
    count, rows, cols = chunks.shape
    vmem = pl.BlockSpec(memory_space=pltpu.VMEM)
    return pl.pallas_call(
        functools.partial(weight_kernel, nf),
        out_shape=jax.ShapeDtypeStruct((count, rows, cols), chunks.dtype),
        in_specs=[vmem],
        out_specs=vmem,
        scratch_shapes=[
            pltpu.VMEM((nf, rows, cols), chunks.dtype),
            pltpu.VMEM((rows, cols), chunks.dtype),
            pltpu.VMEM((nf, rows, cols), chunks.dtype),
        ]
        + [pltpu.SemaphoreType.DMA((nf,))] * 4,
        compiler_params=pltpu.CompilerParams(collective_id=0, has_side_effects=True),
    )(chunks)


def reduce_sums(sums, nf, ns):
    vmem = pl.BlockSpec(memory_space=pltpu.VMEM)
    return pl.pallas_call(
        functools.partial(sums_kernel, nf, ns),
        out_shape=jax.ShapeDtypeStruct(sums.shape, jnp.float32),
        in_specs=[vmem],
        out_specs=vmem,
        scratch_shapes=[
            pltpu.VMEM((nf,) + sums.shape, jnp.float32),
            pltpu.VMEM(sums.shape, jnp.float32),
            pltpu.VMEM((ns,) + sums.shape, jnp.float32),
        ]
        + [pltpu.SemaphoreType.DMA((nf,)), pltpu.SemaphoreType.DMA((nf,))]
        + [pltpu.SemaphoreType.DMA((ns,)), pltpu.SemaphoreType.DMA((ns,))],
        compiler_params=pltpu.CompilerParams(collective_id=1, has_side_effects=True),
    )(sums)


def per_device(
    hidden_in, attn_cotangent, w_qkv, modulation_table, snr_table, timestep, weight_index
):
    clip_count, frame_dev, row_dev, col_count, model_width = hidden_in.shape
    frame_n = lax.axis_size("frame")
    space_n = lax.axis_size("space")
    positions = row_dev * col_count
    w_full = lax.all_gather(w_qkv, "space", axis=0, tiled=True)
    both = jnp.stack(
        [
            hidden_in.reshape(clip_count, frame_dev, positions, model_width),
            attn_cotangent.reshape(clip_count, frame_dev, positions, model_width),
        ],
        axis=3,
    )
    both = lax.all_to_all(both, "frame", split_axis=2, concat_axis=1, tiled=True)
    frames = both.shape[1]
    across = both.shape[2]
    values_in = both[:, :, :, 0].astype(jnp.float32)
    average = jnp.mean(values_in, axis=-1, keepdims=True)
    centered = values_in - average
    variance = jnp.mean(centered * centered, axis=-1, keepdims=True)
    inverse_std = lax.rsqrt(variance + 1e-06)
    normed = centered * inverse_std
    modulation = modulation_table[timestep].astype(jnp.float32)
    shift = modulation[:, 0][:, None, None, :]
    scale = modulation[:, 1][:, None, None, :]
    modulated = (normed * (1.0 + scale) + shift).astype(jnp.bfloat16)
    mod_rows = modulated.reshape(-1, model_width)
    projected = jnp.dot(mod_rows, w_full, preferred_element_type=jnp.float32).astype(jnp.bfloat16)
    pieces = projected.reshape(clip_count, frames, across, 3, HEADS, HEAD_DIM)
    loss_weight = snr_table[weight_index]
    upstream = (
        loss_weight[:, None, None, None] * both[:, :, :, 1].astype(jnp.float32)
    ).astype(jnp.bfloat16)
    upstream = upstream.reshape(clip_count, frames, across, HEADS, HEAD_DIM)
    head_grads = attend_back(pieces[:, :, :, 0], pieces[:, :, :, 1], pieces[:, :, :, 2], upstream)
    grad_rows = jnp.stack(head_grads, axis=3).reshape(-1, 3 * model_width)
    grad_scale_factor = float(mod_rows.shape[0] * frame_n * space_n) ** (-0.5)
    term = lax.dot_general(
        mod_rows, grad_rows, (((0,), (0,)), ((), ())), preferred_element_type=jnp.float32
    ).astype(jnp.bfloat16)
    col_blk = 3 * model_width // frame_n
    share = lax.psum_scatter(term, "space", scatter_dimension=0, tiled=True)
    row_blk = share.shape[0]
    share = share.reshape(row_blk, frame_n, col_blk).transpose(1, 0, 2)
    grad_hidden = lax.dot_general(
        grad_rows, w_full, (((1,), (1,)), ((), ())), preferred_element_type=jnp.float32
    )
    grad_hidden = grad_hidden.reshape(values_in.shape)
    local_sums = jnp.stack(
        [jnp.sum(grad_hidden, axis=(1, 2)), jnp.sum(grad_hidden * normed, axis=(1, 2))],
        axis=1,
    )
    local_sums = local_sums.reshape(-1, model_width)
    gm = reduce_sums(local_sums, frame_n, space_n)
    gw = reduce_weight(share, frame_n).astype(jnp.float32)
    grad_weight = gw.transpose(1, 0, 2).reshape(row_blk, 3 * model_width) * grad_scale_factor
    grad_modulation = gm.reshape(clip_count, 2, model_width) * grad_scale_factor
    grad_normed = grad_hidden * (1.0 + scale)
    grad_input = (
        grad_normed
        - jnp.mean(grad_normed, axis=-1, keepdims=True)
        - normed * jnp.mean(grad_normed * normed, axis=-1, keepdims=True)
    ) * inverse_std
    grad_input = grad_input.astype(jnp.bfloat16)
    grad_input = lax.all_to_all(grad_input, "frame", split_axis=1, concat_axis=2, tiled=True)
    grad_input = grad_input.reshape(clip_count, frame_dev, row_dev, col_count, model_width)
    return (grad_input, grad_weight, grad_modulation)


def solution(mesh):
    in_specs = (
        P(None, "frame", "space", None, None),
        P(None, "frame", "space", None, None),
        P("space", None),
        P(),
        P(),
        P(),
        P(),
    )
    out_specs = (P(None, "frame", "space", None, None), P("space", None), P())
    return jax.shard_map(
        per_device, mesh=mesh, in_specs=in_specs, out_specs=out_specs, check_vma=False
    )
```

```python
import functools

import jax
import jax.numpy as jnp
from jax import lax
from jax.experimental import pallas as pl
from jax.experimental.pallas import tpu as pltpu
from jax.sharding import PartitionSpec as P

MESH = pl.DeviceIdType.MESH

HEADS = 16
HEAD_DIM = 72


def attend_back(queries, keys, values, upstream):
    factor = queries.shape[-1] ** (-0.5)
    queries = queries.astype(jnp.float32)
    keys = keys.astype(jnp.float32)
    values = values.astype(jnp.float32)
    upstream = upstream.astype(jnp.float32)
    highest = lax.Precision.HIGHEST
    scores = jnp.einsum("bfxhe,bgxhe->bxhfg", queries, keys, precision=highest) * factor
    expd = jnp.exp(scores)
    probs = expd / jnp.sum(expd, axis=-1, keepdims=True)
    grad_probs = jnp.einsum("bfxhe,bgxhe->bxhfg", upstream, values, precision=highest)
    grad_values = jnp.einsum("bxhfg,bfxhe->bgxhe", probs, upstream, precision=highest)
    grad_scores = probs * (grad_probs - jnp.sum(probs * grad_probs, axis=-1, keepdims=True))
    grad_queries = jnp.einsum("bxhfg,bgxhe->bfxhe", grad_scores, keys, precision=highest) * factor
    grad_keys = jnp.einsum("bxhfg,bfxhe->bgxhe", grad_scores, queries, precision=highest) * factor
    return (
        grad_queries.astype(jnp.bfloat16),
        grad_keys.astype(jnp.bfloat16),
        grad_values.astype(jnp.bfloat16),
    )


def barrier_with(peers):
    barrier = pltpu.get_barrier_semaphore()
    for p in peers:
        pl.semaphore_signal(barrier, inc=1, device_id=p, device_id_type=MESH)
    pl.semaphore_wait(barrier, len(peers))


def exchange(src_ref, dst, peer_of, index_of, count, send_sem, recv_sem):
    sends = []
    for k in range(1, count):
        t = lax.rem(index_of + k, count)
        c = pltpu.make_async_remote_copy(
            src_ref=src_ref(t), dst_ref=dst.at[index_of], send_sem=send_sem.at[k],
            recv_sem=recv_sem.at[index_of], device_id=peer_of(t), device_id_type=MESH,
        )
        c.start()
        sends.append(c)
    return sends


def wait_all(src_ref, dst, peer_of, index_of, count, send_sem, recv_sem, sends):
    for k in range(1, count):
        src = lax.rem(index_of + count - k, count)
        pltpu.make_async_remote_copy(
            src_ref=src_ref(0), dst_ref=dst.at[src], send_sem=send_sem.at[k],
            recv_sem=recv_sem.at[src], device_id=peer_of(src), device_id_type=MESH,
        ).wait_recv()
    for c in sends:
        c.wait_send()


def weight_kernel(nf, chunks_ref, gw_ref, recv1, redbuf, recv2, s1, r1, s2, r2):
    me_f = lax.axis_index("frame")
    me_s = lax.axis_index("space")
    peer = lambda t: (t, me_s)
    barrier_with([peer(lax.rem(me_f + k, nf)) for k in range(1, nf)])
    first = lambda t: chunks_ref.at[t]
    sends = exchange(first, recv1, peer, me_f, nf, s1, r1)
    recv1[me_f] = chunks_ref[me_f]
    wait_all(first, recv1, peer, me_f, nf, s1, r1, sends)
    acc = recv1[0].astype(jnp.float32)
    for j in range(1, nf):
        acc = acc + recv1[j].astype(jnp.float32)
    acc = acc.astype(redbuf.dtype)
    redbuf[...] = acc
    recv2[me_f] = acc
    second = lambda t: redbuf
    sends = exchange(second, recv2, peer, me_f, nf, s2, r2)
    wait_all(second, recv2, peer, me_f, nf, s2, r2, sends)
    gw_ref[...] = recv2[...]


def sums_kernel(nf, ns, sums_ref, gm_ref, msum1, mbuf, msum2, s1, r1, s2, r2):
    me_f = lax.axis_index("frame")
    me_s = lax.axis_index("space")
    fpeer = lambda t: (t, me_s)
    speer = lambda t: (me_f, t)
    barrier_with(
        [fpeer(lax.rem(me_f + k, nf)) for k in range(1, nf)]
        + [speer(lax.rem(me_s + k, ns)) for k in range(1, ns)]
    )
    first = lambda t: sums_ref
    sends = exchange(first, msum1, fpeer, me_f, nf, s1, r1)
    msum1[me_f] = sums_ref[...]
    wait_all(first, msum1, fpeer, me_f, nf, s1, r1, sends)
    macc = msum1[0]
    for j in range(1, nf):
        macc = macc + msum1[j]
    mbuf[...] = macc
    msum2[me_s] = macc
    second = lambda t: mbuf
    sends = exchange(second, msum2, speer, me_s, ns, s2, r2)
    wait_all(second, msum2, speer, me_s, ns, s2, r2, sends)
    total = msum2[0]
    for j in range(1, ns):
        total = total + msum2[j]
    gm_ref[...] = total


def reduce_weight(chunks, nf, cid):
    count, rows, cols = chunks.shape
    vmem = pl.BlockSpec(memory_space=pltpu.VMEM)
    return pl.pallas_call(
        functools.partial(weight_kernel, nf),
        out_shape=jax.ShapeDtypeStruct((count, rows, cols), chunks.dtype),
        in_specs=[vmem],
        out_specs=vmem,
        scratch_shapes=[
            pltpu.VMEM((nf, rows, cols), chunks.dtype),
            pltpu.VMEM((rows, cols), chunks.dtype),
            pltpu.VMEM((nf, rows, cols), chunks.dtype),
        ]
        + [pltpu.SemaphoreType.DMA((nf,))] * 4,
        compiler_params=pltpu.CompilerParams(collective_id=cid, has_side_effects=True),
    )(chunks)


def reduce_sums(sums, nf, ns):
    vmem = pl.BlockSpec(memory_space=pltpu.VMEM)
    return pl.pallas_call(
        functools.partial(sums_kernel, nf, ns),
        out_shape=jax.ShapeDtypeStruct(sums.shape, jnp.float32),
        in_specs=[vmem],
        out_specs=vmem,
        scratch_shapes=[
            pltpu.VMEM((nf,) + sums.shape, jnp.float32),
            pltpu.VMEM(sums.shape, jnp.float32),
            pltpu.VMEM((ns,) + sums.shape, jnp.float32),
        ]
        + [pltpu.SemaphoreType.DMA((nf,)), pltpu.SemaphoreType.DMA((nf,))]
        + [pltpu.SemaphoreType.DMA((ns,)), pltpu.SemaphoreType.DMA((ns,))],
        compiler_params=pltpu.CompilerParams(collective_id=1, has_side_effects=True),
    )(sums)


def per_device(
    hidden_in, attn_cotangent, w_qkv, modulation_table, snr_table, timestep, weight_index
):
    clip_count, frame_dev, row_dev, col_count, model_width = hidden_in.shape
    frame_n = lax.axis_size("frame")
    space_n = lax.axis_size("space")
    positions = row_dev * col_count
    w_full = lax.all_gather(w_qkv, "space", axis=0, tiled=True)
    both = jnp.stack(
        [
            hidden_in.reshape(clip_count, frame_dev, positions, model_width),
            attn_cotangent.reshape(clip_count, frame_dev, positions, model_width),
        ],
        axis=3,
    )
    both = lax.all_to_all(both, "frame", split_axis=2, concat_axis=1, tiled=True)
    frames = both.shape[1]
    across = both.shape[2]
    values_in = both[:, :, :, 0].astype(jnp.float32)
    average = jnp.mean(values_in, axis=-1, keepdims=True)
    centered = values_in - average
    variance = jnp.mean(centered * centered, axis=-1, keepdims=True)
    inverse_std = lax.rsqrt(variance + 1e-06)
    normed = centered * inverse_std
    modulation = modulation_table[timestep].astype(jnp.float32)
    shift = modulation[:, 0][:, None, None, :]
    scale = modulation[:, 1][:, None, None, :]
    modulated = (normed * (1.0 + scale) + shift).astype(jnp.bfloat16)
    mod_rows = modulated.reshape(-1, model_width)
    projected = jnp.dot(mod_rows, w_full, preferred_element_type=jnp.float32).astype(jnp.bfloat16)
    pieces = projected.reshape(clip_count, frames, across, 3, HEADS, HEAD_DIM)
    loss_weight = snr_table[weight_index]
    upstream = (
        loss_weight[:, None, None, None] * both[:, :, :, 1].astype(jnp.float32)
    ).astype(jnp.bfloat16)
    upstream = upstream.reshape(clip_count, frames, across, HEADS, HEAD_DIM)
    head_grads = attend_back(pieces[:, :, :, 0], pieces[:, :, :, 1], pieces[:, :, :, 2], upstream)
    grad_rows = jnp.stack(head_grads, axis=3).reshape(-1, 3 * model_width)
    grad_scale_factor = float(mod_rows.shape[0] * frame_n * space_n) ** (-0.5)
    row_blk = model_width // space_n

    def reduce_columns(grads, cid):
        cols = grads.shape[1]
        term = lax.dot_general(
            mod_rows, grads, (((0,), (0,)), ((), ())), preferred_element_type=jnp.float32
        ).astype(jnp.bfloat16)
        share = lax.psum_scatter(term, "space", scatter_dimension=0, tiled=True)
        share = share.reshape(row_blk, frame_n, cols // frame_n).transpose(1, 0, 2)
        gw = reduce_weight(share, frame_n, cid).astype(jnp.float32)
        return gw.transpose(1, 0, 2).reshape(row_blk, cols)

    gv_rows = head_grads[2].reshape(-1, model_width)
    gqk_rows = jnp.stack(head_grads[:2], axis=3).reshape(-1, 2 * model_width)
    gw_v = reduce_columns(gv_rows, 2)
    gw_qk = reduce_columns(gqk_rows, 0)
    grad_weight = jnp.concatenate([gw_qk, gw_v], axis=1) * grad_scale_factor
    grad_hidden = lax.dot_general(
        grad_rows, w_full, (((1,), (1,)), ((), ())), preferred_element_type=jnp.float32
    )
    grad_hidden = grad_hidden.reshape(values_in.shape)
    local_sums = jnp.stack(
        [jnp.sum(grad_hidden, axis=(1, 2)), jnp.sum(grad_hidden * normed, axis=(1, 2))],
        axis=1,
    )
    local_sums = local_sums.reshape(-1, model_width)
    gm = reduce_sums(local_sums, frame_n, space_n)
    grad_modulation = gm.reshape(clip_count, 2, model_width) * grad_scale_factor
    grad_normed = grad_hidden * (1.0 + scale)
    grad_input = (
        grad_normed
        - jnp.mean(grad_normed, axis=-1, keepdims=True)
        - normed * jnp.mean(grad_normed * normed, axis=-1, keepdims=True)
    ) * inverse_std
    grad_input = grad_input.astype(jnp.bfloat16)
    grad_input = lax.all_to_all(grad_input, "frame", split_axis=1, concat_axis=2, tiled=True)
    grad_input = grad_input.reshape(clip_count, frame_dev, row_dev, col_count, model_width)
    return (grad_input, grad_weight, grad_modulation)


def solution(mesh):
    in_specs = (
        P(None, "frame", "space", None, None),
        P(None, "frame", "space", None, None),
        P("space", None),
        P(),
        P(),
        P(),
        P(),
    )
    out_specs = (P(None, "frame", "space", None, None), P("space", None), P())
    return jax.shard_map(
        per_device, mesh=mesh, in_specs=in_specs, out_specs=out_specs, check_vma=False
    )
```

```python
import functools

import jax
import jax.numpy as jnp
from jax import lax
from jax.experimental import pallas as pl
from jax.experimental.pallas import tpu as pltpu
from jax.sharding import PartitionSpec as P

MESH = pl.DeviceIdType.MESH

HEADS = 16
HEAD_DIM = 72


def attend_back(queries, keys, values, upstream):
    factor = queries.shape[-1] ** (-0.5)
    queries = queries.astype(jnp.float32)
    keys = keys.astype(jnp.float32)
    values = values.astype(jnp.float32)
    upstream = upstream.astype(jnp.float32)
    highest = lax.Precision.HIGHEST
    scores = jnp.einsum("bfxhe,bgxhe->bxhfg", queries, keys, precision=highest) * factor
    expd = jnp.exp(scores)
    probs = expd / jnp.sum(expd, axis=-1, keepdims=True)
    grad_probs = jnp.einsum("bfxhe,bgxhe->bxhfg", upstream, values, precision=highest)
    grad_values = jnp.einsum("bxhfg,bfxhe->bgxhe", probs, upstream, precision=highest)
    grad_scores = probs * (grad_probs - jnp.sum(probs * grad_probs, axis=-1, keepdims=True))
    grad_queries = jnp.einsum("bxhfg,bgxhe->bfxhe", grad_scores, keys, precision=highest) * factor
    grad_keys = jnp.einsum("bxhfg,bfxhe->bgxhe", grad_scores, queries, precision=highest) * factor
    return (
        grad_queries.astype(jnp.bfloat16),
        grad_keys.astype(jnp.bfloat16),
        grad_values.astype(jnp.bfloat16),
    )


def barrier_with(peers):
    barrier = pltpu.get_barrier_semaphore()
    for p in peers:
        pl.semaphore_signal(barrier, inc=1, device_id=p, device_id_type=MESH)
    pl.semaphore_wait(barrier, len(peers))


def exchange(src_ref, dst, peer_of, index_of, count, send_sem, recv_sem):
    sends = []
    for k in range(1, count):
        t = lax.rem(index_of + k, count)
        c = pltpu.make_async_remote_copy(
            src_ref=src_ref(t), dst_ref=dst.at[index_of], send_sem=send_sem.at[k],
            recv_sem=recv_sem.at[index_of], device_id=peer_of(t), device_id_type=MESH,
        )
        c.start()
        sends.append(c)
    return sends


def wait_all(src_ref, dst, peer_of, index_of, count, send_sem, recv_sem, sends):
    for k in range(1, count):
        src = lax.rem(index_of + count - k, count)
        pltpu.make_async_remote_copy(
            src_ref=src_ref(0), dst_ref=dst.at[src], send_sem=send_sem.at[k],
            recv_sem=recv_sem.at[src], device_id=peer_of(src), device_id_type=MESH,
        ).wait_recv()
    for c in sends:
        c.wait_send()


def space_parts(sub, s):
    nz, nx, nc = sub
    return (s // (nx * nc), lax.rem(s // nc, nx), lax.rem(s, nc))


def space_index(sub):
    nz, nx, nc = sub
    return (lax.axis_index("sz") * nx + lax.axis_index("sx")) * nc + lax.axis_index("sc")


def weight_kernel(nf, sub, chunks_ref, gw_ref, recv1, redbuf, recv2, s1, r1, s2, r2):
    me_f = lax.axis_index("frame")
    here = space_parts(sub, space_index(sub))
    peer = lambda t: (t,) + here
    barrier_with([peer(lax.rem(me_f + k, nf)) for k in range(1, nf)])
    first = lambda t: chunks_ref.at[t]
    sends = exchange(first, recv1, peer, me_f, nf, s1, r1)
    recv1[me_f] = chunks_ref[me_f]
    wait_all(first, recv1, peer, me_f, nf, s1, r1, sends)
    acc = recv1[0].astype(jnp.float32)
    for j in range(1, nf):
        acc = acc + recv1[j].astype(jnp.float32)
    acc = acc.astype(redbuf.dtype)
    redbuf[...] = acc
    recv2[me_f] = acc
    second = lambda t: redbuf
    sends = exchange(second, recv2, peer, me_f, nf, s2, r2)
    wait_all(second, recv2, peer, me_f, nf, s2, r2, sends)
    gw_ref[...] = recv2[...]


def sums_kernel(nf, sub, sums_ref, gm_ref, msum1, mbuf, msum2, s1, r1, s2, r2):
    ns = sub[0] * sub[1] * sub[2]
    me_f = lax.axis_index("frame")
    me_s = space_index(sub)
    fpeer = lambda t: (t,) + space_parts(sub, me_s)
    speer = lambda t: (me_f,) + space_parts(sub, t)
    barrier_with(
        [fpeer(lax.rem(me_f + k, nf)) for k in range(1, nf)]
        + [speer(lax.rem(me_s + k, ns)) for k in range(1, ns)]
    )
    first = lambda t: sums_ref
    sends = exchange(first, msum1, fpeer, me_f, nf, s1, r1)
    msum1[me_f] = sums_ref[...]
    wait_all(first, msum1, fpeer, me_f, nf, s1, r1, sends)
    macc = msum1[0]
    for j in range(1, nf):
        macc = macc + msum1[j]
    mbuf[...] = macc
    msum2[me_s] = macc
    second = lambda t: mbuf
    sends = exchange(second, msum2, speer, me_s, ns, s2, r2)
    wait_all(second, msum2, speer, me_s, ns, s2, r2, sends)
    total = msum2[0]
    for j in range(1, ns):
        total = total + msum2[j]
    gm_ref[...] = total


def reduce_weight(chunks, nf, sub):
    count, rows, cols = chunks.shape
    vmem = pl.BlockSpec(memory_space=pltpu.VMEM)
    return pl.pallas_call(
        functools.partial(weight_kernel, nf, sub),
        out_shape=jax.ShapeDtypeStruct((count, rows, cols), chunks.dtype),
        in_specs=[vmem],
        out_specs=vmem,
        scratch_shapes=[
            pltpu.VMEM((nf, rows, cols), chunks.dtype),
            pltpu.VMEM((rows, cols), chunks.dtype),
            pltpu.VMEM((nf, rows, cols), chunks.dtype),
        ]
        + [pltpu.SemaphoreType.DMA((nf,))] * 4,
        compiler_params=pltpu.CompilerParams(collective_id=0, has_side_effects=True),
    )(chunks)


def reduce_sums(sums, nf, sub):
    ns = sub[0] * sub[1] * sub[2]
    vmem = pl.BlockSpec(memory_space=pltpu.VMEM)
    return pl.pallas_call(
        functools.partial(sums_kernel, nf, sub),
        out_shape=jax.ShapeDtypeStruct(sums.shape, jnp.float32),
        in_specs=[vmem],
        out_specs=vmem,
        scratch_shapes=[
            pltpu.VMEM((nf,) + sums.shape, jnp.float32),
            pltpu.VMEM(sums.shape, jnp.float32),
            pltpu.VMEM((ns,) + sums.shape, jnp.float32),
        ]
        + [pltpu.SemaphoreType.DMA((nf,)), pltpu.SemaphoreType.DMA((nf,))]
        + [pltpu.SemaphoreType.DMA((ns,)), pltpu.SemaphoreType.DMA((ns,))],
        compiler_params=pltpu.CompilerParams(collective_id=1, has_side_effects=True),
    )(sums)


def per_device(
    hidden_in, attn_cotangent, w_qkv, modulation_table, snr_table, timestep, weight_index
):
    clip_count, frame_dev, row_dev, col_count, model_width = hidden_in.shape
    frame_n = lax.axis_size("frame")
    sub = (lax.axis_size("sz"), lax.axis_size("sx"), lax.axis_size("sc"))
    space_n = sub[0] * sub[1] * sub[2]
    positions = row_dev * col_count
    w_full = lax.all_gather(w_qkv, ("sz", "sx", "sc"), axis=0, tiled=True)
    both = jnp.stack(
        [
            hidden_in.reshape(clip_count, frame_dev, positions, model_width),
            attn_cotangent.reshape(clip_count, frame_dev, positions, model_width),
        ],
        axis=3,
    )
    both = lax.all_to_all(both, "frame", split_axis=2, concat_axis=1, tiled=True)
    frames = both.shape[1]
    across = both.shape[2]
    values_in = both[:, :, :, 0].astype(jnp.float32)
    average = jnp.mean(values_in, axis=-1, keepdims=True)
    centered = values_in - average
    variance = jnp.mean(centered * centered, axis=-1, keepdims=True)
    inverse_std = lax.rsqrt(variance + 1e-06)
    normed = centered * inverse_std
    modulation = modulation_table[timestep].astype(jnp.float32)
    shift = modulation[:, 0][:, None, None, :]
    scale = modulation[:, 1][:, None, None, :]
    modulated = (normed * (1.0 + scale) + shift).astype(jnp.bfloat16)
    mod_rows = modulated.reshape(-1, model_width)
    projected = jnp.dot(mod_rows, w_full, preferred_element_type=jnp.float32).astype(jnp.bfloat16)
    pieces = projected.reshape(clip_count, frames, across, 3, HEADS, HEAD_DIM)
    loss_weight = snr_table[weight_index]
    upstream = (
        loss_weight[:, None, None, None] * both[:, :, :, 1].astype(jnp.float32)
    ).astype(jnp.bfloat16)
    upstream = upstream.reshape(clip_count, frames, across, HEADS, HEAD_DIM)
    head_grads = attend_back(pieces[:, :, :, 0], pieces[:, :, :, 1], pieces[:, :, :, 2], upstream)
    grad_rows = jnp.stack(head_grads, axis=3).reshape(-1, 3 * model_width)
    grad_scale_factor = float(mod_rows.shape[0] * frame_n * space_n) ** (-0.5)
    term = lax.dot_general(
        mod_rows, grad_rows, (((0,), (0,)), ((), ())), preferred_element_type=jnp.float32
    ).astype(jnp.bfloat16)
    col_blk = 3 * model_width // frame_n
    nz, nx, nc = sub
    row_blk = model_width // space_n
    share = term.reshape(nz, nx, nc, row_blk, 3 * model_width)
    share = lax.all_to_all(share, "sc", split_axis=2, concat_axis=2, tiled=True)
    share = jnp.sum(share.astype(jnp.float32), axis=2).astype(jnp.bfloat16)
    share = share.reshape(nz * nx, row_blk, 3 * model_width)
    share = lax.all_to_all(share, ("sz", "sx"), split_axis=0, concat_axis=0, tiled=True)
    share = jnp.sum(share.astype(jnp.float32), axis=0).astype(jnp.bfloat16)
    share = share.reshape(row_blk, frame_n, col_blk).transpose(1, 0, 2)
    gw = reduce_weight(share, frame_n, sub).astype(jnp.float32)
    grad_weight = gw.transpose(1, 0, 2).reshape(row_blk, 3 * model_width) * grad_scale_factor
    grad_hidden = lax.dot_general(
        grad_rows, w_full, (((1,), (1,)), ((), ())), preferred_element_type=jnp.float32
    )
    grad_hidden = grad_hidden.reshape(values_in.shape)
    local_sums = jnp.stack(
        [jnp.sum(grad_hidden, axis=(1, 2)), jnp.sum(grad_hidden * normed, axis=(1, 2))],
        axis=1,
    )
    local_sums = local_sums.reshape(-1, model_width)
    gm = reduce_sums(local_sums, frame_n, sub)
    grad_modulation = gm.reshape(clip_count, 2, model_width) * grad_scale_factor
    grad_normed = grad_hidden * (1.0 + scale)
    grad_input = (
        grad_normed
        - jnp.mean(grad_normed, axis=-1, keepdims=True)
        - normed * jnp.mean(grad_normed * normed, axis=-1, keepdims=True)
    ) * inverse_std
    grad_input = grad_input.astype(jnp.bfloat16)
    grad_input = lax.all_to_all(grad_input, "frame", split_axis=1, concat_axis=2, tiled=True)
    grad_input = grad_input.reshape(clip_count, frame_dev, row_dev, col_count, model_width)
    return (grad_input, grad_weight, grad_modulation)


def solution(mesh):
    space_sub = (2, 4, 2)
    devices = mesh.devices.reshape((mesh.shape["frame"],) + space_sub)
    fine = jax.sharding.Mesh(devices, ("frame", "sz", "sx", "sc"))
    space = ("sz", "sx", "sc")
    in_specs = (
        P(None, "frame", space, None, None),
        P(None, "frame", space, None, None),
        P(space, None),
        P(),
        P(),
        P(),
        P(),
    )
    out_specs = (P(None, "frame", space, None, None), P(space, None), P())
    return jax.shard_map(
        per_device, mesh=fine, in_specs=in_specs, out_specs=out_specs, check_vma=False
    )
```

```python
import functools

import jax
import jax.numpy as jnp
from jax import lax
from jax.experimental import pallas as pl
from jax.experimental.pallas import tpu as pltpu
from jax.sharding import PartitionSpec as P

MESH = pl.DeviceIdType.MESH
FRAME_SUB = (4, 4)

HEADS = 16
HEAD_DIM = 72


def attend_back(queries, keys, values, upstream):
    factor = queries.shape[-1] ** (-0.5)
    queries = queries.astype(jnp.float32)
    keys = keys.astype(jnp.float32)
    values = values.astype(jnp.float32)
    upstream = upstream.astype(jnp.float32)
    highest = lax.Precision.HIGHEST
    scores = jnp.einsum("bfxhe,bgxhe->bxhfg", queries, keys, precision=highest) * factor
    expd = jnp.exp(scores)
    probs = expd / jnp.sum(expd, axis=-1, keepdims=True)
    grad_probs = jnp.einsum("bfxhe,bgxhe->bxhfg", upstream, values, precision=highest)
    grad_values = jnp.einsum("bxhfg,bfxhe->bgxhe", probs, upstream, precision=highest)
    grad_scores = probs * (grad_probs - jnp.sum(probs * grad_probs, axis=-1, keepdims=True))
    grad_queries = jnp.einsum("bxhfg,bgxhe->bfxhe", grad_scores, keys, precision=highest) * factor
    grad_keys = jnp.einsum("bxhfg,bfxhe->bgxhe", grad_scores, queries, precision=highest) * factor
    return (
        grad_queries.astype(jnp.bfloat16),
        grad_keys.astype(jnp.bfloat16),
        grad_values.astype(jnp.bfloat16),
    )


def barrier_with(peers):
    barrier = pltpu.get_barrier_semaphore()
    for p in peers:
        pl.semaphore_signal(barrier, inc=1, device_id=p, device_id_type=MESH)
    pl.semaphore_wait(barrier, len(peers))


def exchange(src_ref, dst, peer_of, index_of, count, send_sem, recv_sem):
    sends = []
    for k in range(1, count):
        t = lax.rem(index_of + k, count)
        c = pltpu.make_async_remote_copy(
            src_ref=src_ref(t), dst_ref=dst.at[index_of], send_sem=send_sem.at[k],
            recv_sem=recv_sem.at[index_of], device_id=peer_of(t), device_id_type=MESH,
        )
        c.start()
        sends.append(c)
    return sends


def wait_all(src_ref, dst, peer_of, index_of, count, send_sem, recv_sem, sends):
    for k in range(1, count):
        src = lax.rem(index_of + count - k, count)
        pltpu.make_async_remote_copy(
            src_ref=src_ref(0), dst_ref=dst.at[src], send_sem=send_sem.at[k],
            recv_sem=recv_sem.at[src], device_id=peer_of(src), device_id_type=MESH,
        ).wait_recv()
    for c in sends:
        c.wait_send()


def weight_kernel(
    nzh, ny, chunks_ref, out_ref, a_recv, partbuf, b_recv, redbuf, c_recv, sems
):
    me_f = lax.axis_index("frame")
    me_s = lax.axis_index("space")
    my_y = lax.rem(me_f, ny)
    my_z = me_f // ny
    ypeer = lambda t: (my_z * ny + t, me_s)
    zpeer = lambda t: (t * ny + my_y, me_s)
    barrier_with(
        [ypeer(lax.rem(my_y + k, ny)) for k in range(1, ny)]
        + [zpeer(lax.rem(my_z + k, nzh)) for k in range(1, nzh)]
    )
    s = [sems.at[i] for i in range(8)]
    first = lambda t: chunks_ref.at[t]
    sends = exchange(first, a_recv, ypeer, my_y, ny, s[0], s[1])
    a_recv[my_y] = chunks_ref[my_y]
    wait_all(first, a_recv, ypeer, my_y, ny, s[0], s[1], sends)
    part = a_recv[0].astype(jnp.float32)
    for j in range(1, ny):
        part = part + a_recv[j].astype(jnp.float32)
    partbuf[...] = part
    second = lambda t: partbuf.at[t]
    sends = exchange(second, b_recv, zpeer, my_z, nzh, s[2], s[3])
    b_recv[my_z] = partbuf[my_z]
    wait_all(second, b_recv, zpeer, my_z, nzh, s[2], s[3], sends)
    red = b_recv[0]
    for j in range(1, nzh):
        red = red + b_recv[j]
    redbuf[...] = red
    third = lambda t: redbuf
    sends = exchange(third, c_recv, zpeer, my_z, nzh, s[4], s[5])
    c_recv[my_z] = red
    wait_all(third, c_recv, zpeer, my_z, nzh, s[4], s[5], sends)
    fourth = lambda t: c_recv
    sends = exchange(fourth, out_ref, ypeer, my_y, ny, s[6], s[7])
    out_ref[my_y] = c_recv[...]
    wait_all(fourth, out_ref, ypeer, my_y, ny, s[6], s[7], sends)


def sums_kernel(nf, ns, sums_ref, gm_ref, msum1, mbuf, msum2, s1, r1, s2, r2):
    me_f = lax.axis_index("frame")
    me_s = lax.axis_index("space")
    fpeer = lambda t: (t, me_s)
    speer = lambda t: (me_f, t)
    barrier_with(
        [fpeer(lax.rem(me_f + k, nf)) for k in range(1, nf)]
        + [speer(lax.rem(me_s + k, ns)) for k in range(1, ns)]
    )
    first = lambda t: sums_ref
    sends = exchange(first, msum1, fpeer, me_f, nf, s1, r1)
    msum1[me_f] = sums_ref[...]
    wait_all(first, msum1, fpeer, me_f, nf, s1, r1, sends)
    macc = msum1[0]
    for j in range(1, nf):
        macc = macc + msum1[j]
    mbuf[...] = macc
    msum2[me_s] = macc
    second = lambda t: mbuf
    sends = exchange(second, msum2, speer, me_s, ns, s2, r2)
    wait_all(second, msum2, speer, me_s, ns, s2, r2, sends)
    total = msum2[0]
    for j in range(1, ns):
        total = total + msum2[j]
    gm_ref[...] = total


def reduce_weight(chunks, nzh, ny):
    rows, cols = chunks.shape[2:]
    vmem = pl.BlockSpec(memory_space=pltpu.VMEM)
    return pl.pallas_call(
        functools.partial(weight_kernel, nzh, ny),
        out_shape=jax.ShapeDtypeStruct((ny, nzh, rows, cols), jnp.float32),
        in_specs=[vmem],
        out_specs=vmem,
        scratch_shapes=[
            pltpu.VMEM((ny, nzh, rows, cols), chunks.dtype),
            pltpu.VMEM((nzh, rows, cols), jnp.float32),
            pltpu.VMEM((nzh, rows, cols), jnp.float32),
            pltpu.VMEM((rows, cols), jnp.float32),
            pltpu.VMEM((nzh, rows, cols), jnp.float32),
            pltpu.SemaphoreType.DMA((8, max(nzh, ny))),
        ],
        compiler_params=pltpu.CompilerParams(collective_id=0, has_side_effects=True),
    )(chunks)


def reduce_sums(sums, nf, ns):
    vmem = pl.BlockSpec(memory_space=pltpu.VMEM)
    return pl.pallas_call(
        functools.partial(sums_kernel, nf, ns),
        out_shape=jax.ShapeDtypeStruct(sums.shape, jnp.float32),
        in_specs=[vmem],
        out_specs=vmem,
        scratch_shapes=[
            pltpu.VMEM((nf,) + sums.shape, jnp.float32),
            pltpu.VMEM(sums.shape, jnp.float32),
            pltpu.VMEM((ns,) + sums.shape, jnp.float32),
        ]
        + [pltpu.SemaphoreType.DMA((nf,)), pltpu.SemaphoreType.DMA((nf,))]
        + [pltpu.SemaphoreType.DMA((ns,)), pltpu.SemaphoreType.DMA((ns,))],
        compiler_params=pltpu.CompilerParams(collective_id=1, has_side_effects=True),
    )(sums)


def per_device(
    hidden_in, attn_cotangent, w_qkv, modulation_table, snr_table, timestep, weight_index
):
    clip_count, frame_dev, row_dev, col_count, model_width = hidden_in.shape
    frame_n = lax.axis_size("frame")
    space_n = lax.axis_size("space")
    positions = row_dev * col_count
    w_full = lax.all_gather(w_qkv, "space", axis=0, tiled=True)
    both = jnp.stack(
        [
            hidden_in.reshape(clip_count, frame_dev, positions, model_width),
            attn_cotangent.reshape(clip_count, frame_dev, positions, model_width),
        ],
        axis=3,
    )
    both = lax.all_to_all(both, "frame", split_axis=2, concat_axis=1, tiled=True)
    frames = both.shape[1]
    across = both.shape[2]
    values_in = both[:, :, :, 0].astype(jnp.float32)
    average = jnp.mean(values_in, axis=-1, keepdims=True)
    centered = values_in - average
    variance = jnp.mean(centered * centered, axis=-1, keepdims=True)
    inverse_std = lax.rsqrt(variance + 1e-06)
    normed = centered * inverse_std
    modulation = modulation_table[timestep].astype(jnp.float32)
    shift = modulation[:, 0][:, None, None, :]
    scale = modulation[:, 1][:, None, None, :]
    modulated = (normed * (1.0 + scale) + shift).astype(jnp.bfloat16)
    mod_rows = modulated.reshape(-1, model_width)
    projected = jnp.dot(mod_rows, w_full, preferred_element_type=jnp.float32).astype(jnp.bfloat16)
    pieces = projected.reshape(clip_count, frames, across, 3, HEADS, HEAD_DIM)
    loss_weight = snr_table[weight_index]
    upstream = (
        loss_weight[:, None, None, None] * both[:, :, :, 1].astype(jnp.float32)
    ).astype(jnp.bfloat16)
    upstream = upstream.reshape(clip_count, frames, across, HEADS, HEAD_DIM)
    head_grads = attend_back(pieces[:, :, :, 0], pieces[:, :, :, 1], pieces[:, :, :, 2], upstream)
    grad_rows = jnp.stack(head_grads, axis=3).reshape(-1, 3 * model_width)
    grad_scale_factor = float(mod_rows.shape[0] * frame_n * space_n) ** (-0.5)
    term = lax.dot_general(
        mod_rows, grad_rows, (((0,), (0,)), ((), ())), preferred_element_type=jnp.float32
    ).astype(jnp.bfloat16)
    col_blk = 3 * model_width // frame_n
    share = lax.psum_scatter(term, "space", scatter_dimension=0, tiled=True)
    row_blk = share.shape[0]
    nzh, ny = FRAME_SUB
    share = share.reshape(row_blk, nzh, ny, col_blk).transpose(2, 1, 0, 3)
    grad_hidden = lax.dot_general(
        grad_rows, w_full, (((1,), (1,)), ((), ())), preferred_element_type=jnp.float32
    )
    grad_hidden = grad_hidden.reshape(values_in.shape)
    local_sums = jnp.stack(
        [jnp.sum(grad_hidden, axis=(1, 2)), jnp.sum(grad_hidden * normed, axis=(1, 2))],
        axis=1,
    )
    local_sums = local_sums.reshape(-1, model_width)
    gm = reduce_sums(local_sums, frame_n, space_n)
    gw = reduce_weight(share, nzh, ny)
    grad_weight = gw.transpose(2, 1, 0, 3).reshape(row_blk, 3 * model_width) * grad_scale_factor
    grad_modulation = gm.reshape(clip_count, 2, model_width) * grad_scale_factor
    grad_normed = grad_hidden * (1.0 + scale)
    grad_input = (
        grad_normed
        - jnp.mean(grad_normed, axis=-1, keepdims=True)
        - normed * jnp.mean(grad_normed * normed, axis=-1, keepdims=True)
    ) * inverse_std
    grad_input = grad_input.astype(jnp.bfloat16)
    grad_input = lax.all_to_all(grad_input, "frame", split_axis=1, concat_axis=2, tiled=True)
    grad_input = grad_input.reshape(clip_count, frame_dev, row_dev, col_count, model_width)
    return (grad_input, grad_weight, grad_modulation)


def solution(mesh):
    in_specs = (
        P(None, "frame", "space", None, None),
        P(None, "frame", "space", None, None),
        P("space", None),
        P(),
        P(),
        P(),
        P(),
    )
    out_specs = (P(None, "frame", "space", None, None), P("space", None), P())
    return jax.shard_map(
        per_device, mesh=mesh, in_specs=in_specs, out_specs=out_specs, check_vma=False
    )
```

```python
import functools

import jax
import jax.numpy as jnp
from jax import lax
from jax.experimental import pallas as pl
from jax.experimental.pallas import tpu as pltpu
from jax.sharding import PartitionSpec as P

MESH = pl.DeviceIdType.MESH

HEADS = 16
HEAD_DIM = 72


def attend_back(queries, keys, values, upstream):
    factor = queries.shape[-1] ** (-0.5)
    queries = queries.astype(jnp.float32)
    keys = keys.astype(jnp.float32)
    values = values.astype(jnp.float32)
    upstream = upstream.astype(jnp.float32)
    highest = lax.Precision.HIGHEST
    scores = jnp.einsum("bfxhe,bgxhe->bxhfg", queries, keys, precision=highest) * factor
    expd = jnp.exp(scores)
    probs = expd / jnp.sum(expd, axis=-1, keepdims=True)
    grad_probs = jnp.einsum("bfxhe,bgxhe->bxhfg", upstream, values, precision=highest)
    grad_values = jnp.einsum("bxhfg,bfxhe->bgxhe", probs, upstream, precision=highest)
    grad_scores = probs * (grad_probs - jnp.sum(probs * grad_probs, axis=-1, keepdims=True))
    grad_queries = jnp.einsum("bxhfg,bgxhe->bfxhe", grad_scores, keys, precision=highest) * factor
    grad_keys = jnp.einsum("bxhfg,bfxhe->bgxhe", grad_scores, queries, precision=highest) * factor
    return (
        grad_queries.astype(jnp.bfloat16),
        grad_keys.astype(jnp.bfloat16),
        grad_values.astype(jnp.bfloat16),
    )


def barrier_with(peers):
    barrier = pltpu.get_barrier_semaphore()
    for p in peers:
        pl.semaphore_signal(barrier, inc=1, device_id=p, device_id_type=MESH)
    pl.semaphore_wait(barrier, len(peers))


def exchange(src_ref, dst, peer_of, index_of, count, send_sem, recv_sem):
    sends = []
    for k in range(1, count):
        t = lax.rem(index_of + k, count)
        c = pltpu.make_async_remote_copy(
            src_ref=src_ref(t), dst_ref=dst.at[index_of], send_sem=send_sem.at[k],
            recv_sem=recv_sem.at[index_of], device_id=peer_of(t), device_id_type=MESH,
        )
        c.start()
        sends.append(c)
    return sends


def wait_all(src_ref, dst, peer_of, index_of, count, send_sem, recv_sem, sends):
    for k in range(1, count):
        src = lax.rem(index_of + count - k, count)
        pltpu.make_async_remote_copy(
            src_ref=src_ref(0), dst_ref=dst.at[src], send_sem=send_sem.at[k],
            recv_sem=recv_sem.at[src], device_id=peer_of(src), device_id_type=MESH,
        ).wait_recv()
    for c in sends:
        c.wait_send()


def space_parts(sub, s):
    nz, nx, nc = sub
    return (s // (nx * nc), lax.rem(s // nc, nx), lax.rem(s, nc))


def space_index(sub):
    nz, nx, nc = sub
    return (lax.axis_index("sz") * nx + lax.axis_index("sx")) * nc + lax.axis_index("sc")


def weight_kernel(nf, sub, chunks_ref, gw_ref, recv1, redbuf, recv2, s1, r1, s2, r2):
    me_f = lax.axis_index("frame")
    here = space_parts(sub, space_index(sub))
    peer = lambda t: (t,) + here
    barrier_with([peer(lax.rem(me_f + k, nf)) for k in range(1, nf)])
    first = lambda t: chunks_ref.at[t]
    sends = exchange(first, recv1, peer, me_f, nf, s1, r1)
    recv1[me_f] = chunks_ref[me_f]
    wait_all(first, recv1, peer, me_f, nf, s1, r1, sends)
    acc = recv1[0].astype(jnp.float32)
    for j in range(1, nf):
        acc = acc + recv1[j].astype(jnp.float32)
    acc = acc.astype(redbuf.dtype)
    redbuf[...] = acc
    recv2[me_f] = acc
    second = lambda t: redbuf
    sends = exchange(second, recv2, peer, me_f, nf, s2, r2)
    wait_all(second, recv2, peer, me_f, nf, s2, r2, sends)
    gw_ref[...] = recv2[...]


def sums_kernel(nf, sub, sums_ref, gm_ref, msum1, mbuf, msum2, s1, r1, s2, r2):
    ns = sub[0] * sub[1] * sub[2]
    me_f = lax.axis_index("frame")
    me_s = space_index(sub)
    fpeer = lambda t: (t,) + space_parts(sub, me_s)
    speer = lambda t: (me_f,) + space_parts(sub, t)
    barrier_with(
        [fpeer(lax.rem(me_f + k, nf)) for k in range(1, nf)]
        + [speer(lax.rem(me_s + k, ns)) for k in range(1, ns)]
    )
    first = lambda t: sums_ref
    sends = exchange(first, msum1, fpeer, me_f, nf, s1, r1)
    msum1[me_f] = sums_ref[...]
    wait_all(first, msum1, fpeer, me_f, nf, s1, r1, sends)
    macc = msum1[0]
    for j in range(1, nf):
        macc = macc + msum1[j]
    mbuf[...] = macc
    msum2[me_s] = macc
    second = lambda t: mbuf
    sends = exchange(second, msum2, speer, me_s, ns, s2, r2)
    wait_all(second, msum2, speer, me_s, ns, s2, r2, sends)
    total = msum2[0]
    for j in range(1, ns):
        total = total + msum2[j]
    gm_ref[...] = total


def reduce_weight(chunks, nf, sub):
    count, rows, cols = chunks.shape
    vmem = pl.BlockSpec(memory_space=pltpu.VMEM)
    return pl.pallas_call(
        functools.partial(weight_kernel, nf, sub),
        out_shape=jax.ShapeDtypeStruct((count, rows, cols), chunks.dtype),
        in_specs=[vmem],
        out_specs=vmem,
        scratch_shapes=[
            pltpu.VMEM((nf, rows, cols), chunks.dtype),
            pltpu.VMEM((rows, cols), chunks.dtype),
            pltpu.VMEM((nf, rows, cols), chunks.dtype),
        ]
        + [pltpu.SemaphoreType.DMA((nf,))] * 4,
        compiler_params=pltpu.CompilerParams(collective_id=0, has_side_effects=True),
    )(chunks)


def reduce_sums(sums, nf, sub):
    ns = sub[0] * sub[1] * sub[2]
    vmem = pl.BlockSpec(memory_space=pltpu.VMEM)
    return pl.pallas_call(
        functools.partial(sums_kernel, nf, sub),
        out_shape=jax.ShapeDtypeStruct(sums.shape, jnp.float32),
        in_specs=[vmem],
        out_specs=vmem,
        scratch_shapes=[
            pltpu.VMEM((nf,) + sums.shape, jnp.float32),
            pltpu.VMEM(sums.shape, jnp.float32),
            pltpu.VMEM((ns,) + sums.shape, jnp.float32),
        ]
        + [pltpu.SemaphoreType.DMA((nf,)), pltpu.SemaphoreType.DMA((nf,))]
        + [pltpu.SemaphoreType.DMA((ns,)), pltpu.SemaphoreType.DMA((ns,))],
        compiler_params=pltpu.CompilerParams(collective_id=1, has_side_effects=True),
    )(sums)


def per_device(
    hidden_in, attn_cotangent, w_qkv, modulation_table, snr_table, timestep, weight_index
):
    clip_count, frame_dev, row_dev, col_count, model_width = hidden_in.shape
    frame_n = lax.axis_size("frame")
    sub = (lax.axis_size("sz"), lax.axis_size("sx"), lax.axis_size("sc"))
    space_n = sub[0] * sub[1] * sub[2]
    positions = row_dev * col_count
    w_full = jnp.broadcast_to(w_qkv, (sub[0] * sub[1],) + w_qkv.shape)
    w_full = lax.all_to_all(w_full, ("sz", "sx"), split_axis=0, concat_axis=0, tiled=True)
    w_full = jnp.broadcast_to(w_full[:, None], (sub[0] * sub[1], sub[2]) + w_qkv.shape)
    w_full = lax.all_to_all(w_full, "sc", split_axis=1, concat_axis=1, tiled=True)
    w_full = w_full.reshape(-1, w_qkv.shape[1])
    both = jnp.stack(
        [
            hidden_in.reshape(clip_count, frame_dev, positions, model_width),
            attn_cotangent.reshape(clip_count, frame_dev, positions, model_width),
        ],
        axis=3,
    )
    both = lax.all_to_all(both, "frame", split_axis=2, concat_axis=1, tiled=True)
    frames = both.shape[1]
    across = both.shape[2]
    values_in = both[:, :, :, 0].astype(jnp.float32)
    average = jnp.mean(values_in, axis=-1, keepdims=True)
    centered = values_in - average
    variance = jnp.mean(centered * centered, axis=-1, keepdims=True)
    inverse_std = lax.rsqrt(variance + 1e-06)
    normed = centered * inverse_std
    modulation = modulation_table[timestep].astype(jnp.float32)
    shift = modulation[:, 0][:, None, None, :]
    scale = modulation[:, 1][:, None, None, :]
    modulated = (normed * (1.0 + scale) + shift).astype(jnp.bfloat16)
    mod_rows = modulated.reshape(-1, model_width)
    projected = jnp.dot(mod_rows, w_full, preferred_element_type=jnp.float32).astype(jnp.bfloat16)
    pieces = projected.reshape(clip_count, frames, across, 3, HEADS, HEAD_DIM)
    loss_weight = snr_table[weight_index]
    upstream = (
        loss_weight[:, None, None, None] * both[:, :, :, 1].astype(jnp.float32)
    ).astype(jnp.bfloat16)
    upstream = upstream.reshape(clip_count, frames, across, HEADS, HEAD_DIM)
    head_grads = attend_back(pieces[:, :, :, 0], pieces[:, :, :, 1], pieces[:, :, :, 2], upstream)
    grad_rows = jnp.stack(head_grads, axis=3).reshape(-1, 3 * model_width)
    grad_scale_factor = float(mod_rows.shape[0] * frame_n * space_n) ** (-0.5)
    term = lax.dot_general(
        mod_rows, grad_rows, (((0,), (0,)), ((), ())), preferred_element_type=jnp.float32
    ).astype(jnp.bfloat16)
    col_blk = 3 * model_width // frame_n
    share = lax.psum_scatter(term, ("sz", "sx", "sc"), scatter_dimension=0, tiled=True)
    row_blk = share.shape[0]
    share = share.reshape(row_blk, frame_n, col_blk).transpose(1, 0, 2)
    grad_hidden = lax.dot_general(
        grad_rows, w_full, (((1,), (1,)), ((), ())), preferred_element_type=jnp.float32
    )
    grad_hidden = grad_hidden.reshape(values_in.shape)
    local_sums = jnp.stack(
        [jnp.sum(grad_hidden, axis=(1, 2)), jnp.sum(grad_hidden * normed, axis=(1, 2))],
        axis=1,
    )
    local_sums = local_sums.reshape(-1, model_width)
    gm = reduce_sums(local_sums, frame_n, sub)
    gw = reduce_weight(share, frame_n, sub).astype(jnp.float32)
    grad_weight = gw.transpose(1, 0, 2).reshape(row_blk, 3 * model_width) * grad_scale_factor
    grad_modulation = gm.reshape(clip_count, 2, model_width) * grad_scale_factor
    grad_normed = grad_hidden * (1.0 + scale)
    grad_input = (
        grad_normed
        - jnp.mean(grad_normed, axis=-1, keepdims=True)
        - normed * jnp.mean(grad_normed * normed, axis=-1, keepdims=True)
    ) * inverse_std
    grad_input = grad_input.astype(jnp.bfloat16)
    grad_input = lax.all_to_all(grad_input, "frame", split_axis=1, concat_axis=2, tiled=True)
    grad_input = grad_input.reshape(clip_count, frame_dev, row_dev, col_count, model_width)
    return (grad_input, grad_weight, grad_modulation)


def solution(mesh):
    space_sub = (2, 4, 2)
    devices = mesh.devices.reshape((mesh.shape["frame"],) + space_sub)
    fine = jax.sharding.Mesh(devices, ("frame", "sz", "sx", "sc"))
    space = ("sz", "sx", "sc")
    in_specs = (
        P(None, "frame", space, None, None),
        P(None, "frame", space, None, None),
        P(space, None),
        P(),
        P(),
        P(),
        P(),
    )
    out_specs = (P(None, "frame", space, None, None), P(space, None), P())
    return jax.shard_map(
        per_device, mesh=fine, in_specs=in_specs, out_specs=out_specs, check_vma=False
    )
```

```python
import functools

import jax
import jax.numpy as jnp
from jax import lax
from jax.experimental import pallas as pl
from jax.experimental.pallas import tpu as pltpu
from jax.sharding import PartitionSpec as P

MESH = pl.DeviceIdType.MESH

HEADS = 16
HEAD_DIM = 72


def attend_back(queries, keys, values, upstream):
    factor = queries.shape[-1] ** (-0.5)
    f32 = jnp.float32
    high = lax.Precision.HIGH
    scores = jnp.einsum("bfxhe,bgxhe->bxhfg", queries, keys, preferred_element_type=f32) * factor
    expd = jnp.exp(scores)
    probs = expd / jnp.sum(expd, axis=-1, keepdims=True)
    grad_probs = jnp.einsum("bfxhe,bgxhe->bxhfg", upstream, values, preferred_element_type=f32)
    grad_values = jnp.einsum(
        "bxhfg,bfxhe->bgxhe", probs, upstream.astype(f32), precision=high
    )
    grad_scores = probs * (grad_probs - jnp.sum(probs * grad_probs, axis=-1, keepdims=True))
    grad_queries = jnp.einsum(
        "bxhfg,bgxhe->bfxhe", grad_scores, keys.astype(f32), precision=high
    ) * factor
    grad_keys = jnp.einsum(
        "bxhfg,bfxhe->bgxhe", grad_scores, queries.astype(f32), precision=high
    ) * factor
    return (
        grad_queries.astype(jnp.bfloat16),
        grad_keys.astype(jnp.bfloat16),
        grad_values.astype(jnp.bfloat16),
    )


def barrier_with(peers):
    barrier = pltpu.get_barrier_semaphore()
    for p in peers:
        pl.semaphore_signal(barrier, inc=1, device_id=p, device_id_type=MESH)
    pl.semaphore_wait(barrier, len(peers))


def exchange(src_ref, dst, peer_of, index_of, count, send_sem, recv_sem):
    sends = []
    for k in range(1, count):
        t = lax.rem(index_of + k, count)
        c = pltpu.make_async_remote_copy(
            src_ref=src_ref(t), dst_ref=dst.at[index_of], send_sem=send_sem.at[k],
            recv_sem=recv_sem.at[index_of], device_id=peer_of(t), device_id_type=MESH,
        )
        c.start()
        sends.append(c)
    return sends


def wait_all(src_ref, dst, peer_of, index_of, count, send_sem, recv_sem, sends):
    for k in range(1, count):
        src = lax.rem(index_of + count - k, count)
        pltpu.make_async_remote_copy(
            src_ref=src_ref(0), dst_ref=dst.at[src], send_sem=send_sem.at[k],
            recv_sem=recv_sem.at[src], device_id=peer_of(src), device_id_type=MESH,
        ).wait_recv()
    for c in sends:
        c.wait_send()


def weight_kernel(nf, chunks_ref, gw_ref, recv1, redbuf, recv2, s1, r1, s2, r2):
    me_f = lax.axis_index("frame")
    me_s = lax.axis_index("space")
    peer = lambda t: (t, me_s)
    barrier_with([peer(lax.rem(me_f + k, nf)) for k in range(1, nf)])
    first = lambda t: chunks_ref.at[t]
    sends = exchange(first, recv1, peer, me_f, nf, s1, r1)
    recv1[me_f] = chunks_ref[me_f]
    wait_all(first, recv1, peer, me_f, nf, s1, r1, sends)
    acc = recv1[0].astype(jnp.float32)
    for j in range(1, nf):
        acc = acc + recv1[j].astype(jnp.float32)
    acc = acc.astype(redbuf.dtype)
    redbuf[...] = acc
    recv2[me_f] = acc
    second = lambda t: redbuf
    sends = exchange(second, recv2, peer, me_f, nf, s2, r2)
    wait_all(second, recv2, peer, me_f, nf, s2, r2, sends)
    gw_ref[...] = recv2[...]


def sums_kernel(nf, ns, sums_ref, gm_ref, msum1, mbuf, msum2, s1, r1, s2, r2):
    me_f = lax.axis_index("frame")
    me_s = lax.axis_index("space")
    fpeer = lambda t: (t, me_s)
    speer = lambda t: (me_f, t)
    barrier_with(
        [fpeer(lax.rem(me_f + k, nf)) for k in range(1, nf)]
        + [speer(lax.rem(me_s + k, ns)) for k in range(1, ns)]
    )
    first = lambda t: sums_ref
    sends = exchange(first, msum1, fpeer, me_f, nf, s1, r1)
    msum1[me_f] = sums_ref[...]
    wait_all(first, msum1, fpeer, me_f, nf, s1, r1, sends)
    macc = msum1[0]
    for j in range(1, nf):
        macc = macc + msum1[j]
    mbuf[...] = macc
    msum2[me_s] = macc
    second = lambda t: mbuf
    sends = exchange(second, msum2, speer, me_s, ns, s2, r2)
    wait_all(second, msum2, speer, me_s, ns, s2, r2, sends)
    total = msum2[0]
    for j in range(1, ns):
        total = total + msum2[j]
    gm_ref[...] = total


def reduce_weight(chunks, nf):
    count, rows, cols = chunks.shape
    vmem = pl.BlockSpec(memory_space=pltpu.VMEM)
    return pl.pallas_call(
        functools.partial(weight_kernel, nf),
        out_shape=jax.ShapeDtypeStruct((count, rows, cols), chunks.dtype),
        in_specs=[vmem],
        out_specs=vmem,
        scratch_shapes=[
            pltpu.VMEM((nf, rows, cols), chunks.dtype),
            pltpu.VMEM((rows, cols), chunks.dtype),
            pltpu.VMEM((nf, rows, cols), chunks.dtype),
        ]
        + [pltpu.SemaphoreType.DMA((nf,))] * 4,
        compiler_params=pltpu.CompilerParams(collective_id=0, has_side_effects=True),
    )(chunks)


def reduce_sums(sums, nf, ns):
    vmem = pl.BlockSpec(memory_space=pltpu.VMEM)
    return pl.pallas_call(
        functools.partial(sums_kernel, nf, ns),
        out_shape=jax.ShapeDtypeStruct(sums.shape, jnp.float32),
        in_specs=[vmem],
        out_specs=vmem,
        scratch_shapes=[
            pltpu.VMEM((nf,) + sums.shape, jnp.float32),
            pltpu.VMEM(sums.shape, jnp.float32),
            pltpu.VMEM((ns,) + sums.shape, jnp.float32),
        ]
        + [pltpu.SemaphoreType.DMA((nf,)), pltpu.SemaphoreType.DMA((nf,))]
        + [pltpu.SemaphoreType.DMA((ns,)), pltpu.SemaphoreType.DMA((ns,))],
        compiler_params=pltpu.CompilerParams(collective_id=1, has_side_effects=True),
    )(sums)


def per_device(
    hidden_in, attn_cotangent, w_qkv, modulation_table, snr_table, timestep, weight_index
):
    clip_count, frame_dev, row_dev, col_count, model_width = hidden_in.shape
    frame_n = lax.axis_size("frame")
    space_n = lax.axis_size("space")
    positions = row_dev * col_count
    w_full = lax.all_gather(w_qkv, "space", axis=0, tiled=True)
    both = jnp.stack(
        [
            hidden_in.reshape(clip_count, frame_dev, positions, model_width),
            attn_cotangent.reshape(clip_count, frame_dev, positions, model_width),
        ],
        axis=3,
    )
    both = lax.all_to_all(both, "frame", split_axis=2, concat_axis=1, tiled=True)
    frames = both.shape[1]
    across = both.shape[2]
    values_in = both[:, :, :, 0].astype(jnp.float32)
    average = jnp.mean(values_in, axis=-1, keepdims=True)
    centered = values_in - average
    variance = jnp.mean(centered * centered, axis=-1, keepdims=True)
    inverse_std = lax.rsqrt(variance + 1e-06)
    normed = centered * inverse_std
    modulation = modulation_table[timestep].astype(jnp.float32)
    shift = modulation[:, 0][:, None, None, :]
    scale = modulation[:, 1][:, None, None, :]
    modulated = (normed * (1.0 + scale) + shift).astype(jnp.bfloat16)
    mod_rows = modulated.reshape(-1, model_width)
    projected = jnp.dot(mod_rows, w_full, preferred_element_type=jnp.float32).astype(jnp.bfloat16)
    pieces = projected.reshape(clip_count, frames, across, 3, HEADS, HEAD_DIM)
    loss_weight = snr_table[weight_index]
    upstream = (
        loss_weight[:, None, None, None] * both[:, :, :, 1].astype(jnp.float32)
    ).astype(jnp.bfloat16)
    upstream = upstream.reshape(clip_count, frames, across, HEADS, HEAD_DIM)
    head_grads = attend_back(pieces[:, :, :, 0], pieces[:, :, :, 1], pieces[:, :, :, 2], upstream)
    grad_rows = jnp.stack(head_grads, axis=3).reshape(-1, 3 * model_width)
    grad_scale_factor = float(mod_rows.shape[0] * frame_n * space_n) ** (-0.5)
    term = lax.dot_general(
        mod_rows, grad_rows, (((0,), (0,)), ((), ())), preferred_element_type=jnp.float32
    ).astype(jnp.bfloat16)
    col_blk = 3 * model_width // frame_n
    share = lax.psum_scatter(term, "space", scatter_dimension=0, tiled=True)
    row_blk = share.shape[0]
    share = share.reshape(row_blk, frame_n, col_blk).transpose(1, 0, 2)
    grad_hidden = lax.dot_general(
        grad_rows, w_full, (((1,), (1,)), ((), ())), preferred_element_type=jnp.float32
    )
    grad_hidden = grad_hidden.reshape(values_in.shape)
    local_sums = jnp.stack(
        [jnp.sum(grad_hidden, axis=(1, 2)), jnp.sum(grad_hidden * normed, axis=(1, 2))],
        axis=1,
    )
    local_sums = local_sums.reshape(-1, model_width)
    gm = reduce_sums(local_sums, frame_n, space_n)
    gw = reduce_weight(share, frame_n).astype(jnp.float32)
    grad_weight = gw.transpose(1, 0, 2).reshape(row_blk, 3 * model_width) * grad_scale_factor
    grad_modulation = gm.reshape(clip_count, 2, model_width) * grad_scale_factor
    grad_normed = grad_hidden * (1.0 + scale)
    grad_input = (
        grad_normed
        - jnp.mean(grad_normed, axis=-1, keepdims=True)
        - normed * jnp.mean(grad_normed * normed, axis=-1, keepdims=True)
    ) * inverse_std
    grad_input = grad_input.astype(jnp.bfloat16)
    grad_input = lax.all_to_all(grad_input, "frame", split_axis=1, concat_axis=2, tiled=True)
    grad_input = grad_input.reshape(clip_count, frame_dev, row_dev, col_count, model_width)
    return (grad_input, grad_weight, grad_modulation)


def solution(mesh):
    in_specs = (
        P(None, "frame", "space", None, None),
        P(None, "frame", "space", None, None),
        P("space", None),
        P(),
        P(),
        P(),
        P(),
    )
    out_specs = (P(None, "frame", "space", None, None), P("space", None), P())
    return jax.shard_map(
        per_device, mesh=mesh, in_specs=in_specs, out_specs=out_specs, check_vma=False
    )
```

```python
import functools

import jax
import jax.numpy as jnp
from jax import lax
from jax.experimental import pallas as pl
from jax.experimental.pallas import tpu as pltpu
from jax.sharding import PartitionSpec as P

MESH = pl.DeviceIdType.MESH

HEADS = 16
HEAD_DIM = 72


def attend_back(queries, keys, values, upstream):
    factor = queries.shape[-1] ** (-0.5)
    f32 = jnp.float32
    high = lax.Precision.HIGH
    scores = jnp.einsum("bfxhe,bgxhe->bxhfg", queries, keys, preferred_element_type=f32) * factor
    expd = jnp.exp(scores)
    probs = expd / jnp.sum(expd, axis=-1, keepdims=True)
    grad_probs = jnp.einsum("bfxhe,bgxhe->bxhfg", upstream, values, preferred_element_type=f32)
    grad_values = jnp.einsum(
        "bxhfg,bfxhe->bgxhe", probs, upstream.astype(f32), precision=high
    )
    grad_scores = probs * (grad_probs - jnp.sum(probs * grad_probs, axis=-1, keepdims=True))
    grad_queries = jnp.einsum(
        "bxhfg,bgxhe->bfxhe", grad_scores, keys.astype(f32), precision=high
    ) * factor
    grad_keys = jnp.einsum(
        "bxhfg,bfxhe->bgxhe", grad_scores, queries.astype(f32), precision=high
    ) * factor
    return (
        grad_queries.astype(jnp.bfloat16),
        grad_keys.astype(jnp.bfloat16),
        grad_values.astype(jnp.bfloat16),
    )


def barrier_with(peers):
    barrier = pltpu.get_barrier_semaphore()
    for p in peers:
        pl.semaphore_signal(barrier, inc=1, device_id=p, device_id_type=MESH)
    pl.semaphore_wait(barrier, len(peers))


def exchange(src_ref, dst, peer_of, index_of, count, send_sem, recv_sem):
    sends = []
    for k in range(1, count):
        t = lax.rem(index_of + k, count)
        c = pltpu.make_async_remote_copy(
            src_ref=src_ref(t), dst_ref=dst.at[index_of], send_sem=send_sem.at[k],
            recv_sem=recv_sem.at[index_of], device_id=peer_of(t), device_id_type=MESH,
        )
        c.start()
        sends.append(c)
    return sends


def wait_all(src_ref, dst, peer_of, index_of, count, send_sem, recv_sem, sends):
    for k in range(1, count):
        src = lax.rem(index_of + count - k, count)
        pltpu.make_async_remote_copy(
            src_ref=src_ref(0), dst_ref=dst.at[src], send_sem=send_sem.at[k],
            recv_sem=recv_sem.at[src], device_id=peer_of(src), device_id_type=MESH,
        ).wait_recv()
    for c in sends:
        c.wait_send()


def weight_kernel(nf, chunks_ref, gw_ref, recv1, redbuf, recv2, s1, r1, s2, r2):
    me_f = lax.axis_index("frame")
    me_s = lax.axis_index("space")
    peer = lambda t: (t, me_s)
    barrier_with([peer(lax.rem(me_f + k, nf)) for k in range(1, nf)])
    first = lambda t: chunks_ref.at[t]
    sends = exchange(first, recv1, peer, me_f, nf, s1, r1)
    recv1[me_f] = chunks_ref[me_f]
    wait_all(first, recv1, peer, me_f, nf, s1, r1, sends)
    acc = recv1[0].astype(jnp.float32)
    for j in range(1, nf):
        acc = acc + recv1[j].astype(jnp.float32)
    acc = acc.astype(redbuf.dtype)
    redbuf[...] = acc
    recv2[me_f] = acc
    second = lambda t: redbuf
    sends = exchange(second, recv2, peer, me_f, nf, s2, r2)
    wait_all(second, recv2, peer, me_f, nf, s2, r2, sends)
    gw_ref[...] = recv2[...]


def sums_kernel(nf, ns, sums_ref, gm_ref, msum1, mbuf, msum2, s1, r1, s2, r2):
    me_f = lax.axis_index("frame")
    me_s = lax.axis_index("space")
    fpeer = lambda t: (t, me_s)
    speer = lambda t: (me_f, t)
    barrier_with(
        [fpeer(lax.rem(me_f + k, nf)) for k in range(1, nf)]
        + [speer(lax.rem(me_s + k, ns)) for k in range(1, ns)]
    )
    first = lambda t: sums_ref
    sends = exchange(first, msum1, fpeer, me_f, nf, s1, r1)
    msum1[me_f] = sums_ref[...]
    wait_all(first, msum1, fpeer, me_f, nf, s1, r1, sends)
    macc = msum1[0]
    for j in range(1, nf):
        macc = macc + msum1[j]
    mbuf[...] = macc
    msum2[me_s] = macc
    second = lambda t: mbuf
    sends = exchange(second, msum2, speer, me_s, ns, s2, r2)
    wait_all(second, msum2, speer, me_s, ns, s2, r2, sends)
    total = msum2[0]
    for j in range(1, ns):
        total = total + msum2[j]
    gm_ref[...] = total


def reduce_weight(chunks, nf):
    count, rows, cols = chunks.shape
    vmem = pl.BlockSpec(memory_space=pltpu.VMEM)
    return pl.pallas_call(
        functools.partial(weight_kernel, nf),
        out_shape=jax.ShapeDtypeStruct((count, rows, cols), chunks.dtype),
        in_specs=[vmem],
        out_specs=vmem,
        scratch_shapes=[
            pltpu.VMEM((nf, rows, cols), chunks.dtype),
            pltpu.VMEM((rows, cols), chunks.dtype),
            pltpu.VMEM((nf, rows, cols), chunks.dtype),
        ]
        + [pltpu.SemaphoreType.DMA((nf,))] * 4,
        compiler_params=pltpu.CompilerParams(collective_id=0, has_side_effects=True),
    )(chunks)


def reduce_sums(sums, nf, ns):
    vmem = pl.BlockSpec(memory_space=pltpu.VMEM)
    return pl.pallas_call(
        functools.partial(sums_kernel, nf, ns),
        out_shape=jax.ShapeDtypeStruct(sums.shape, jnp.float32),
        in_specs=[vmem],
        out_specs=vmem,
        scratch_shapes=[
            pltpu.VMEM((nf,) + sums.shape, jnp.float32),
            pltpu.VMEM(sums.shape, jnp.float32),
            pltpu.VMEM((ns,) + sums.shape, jnp.float32),
        ]
        + [pltpu.SemaphoreType.DMA((nf,)), pltpu.SemaphoreType.DMA((nf,))]
        + [pltpu.SemaphoreType.DMA((ns,)), pltpu.SemaphoreType.DMA((ns,))],
        compiler_params=pltpu.CompilerParams(collective_id=1, has_side_effects=True),
    )(sums)


def per_device(
    hidden_in, attn_cotangent, w_qkv, modulation_table, snr_table, timestep, weight_index
):
    clip_count, frame_dev, row_dev, col_count, model_width = hidden_in.shape
    frame_n = lax.axis_size("frame")
    space_n = lax.axis_size("space")
    positions = row_dev * col_count
    w_full = lax.all_gather(w_qkv, "space", axis=0, tiled=True)
    both = jnp.stack(
        [
            hidden_in.reshape(clip_count, frame_dev, positions, model_width),
            attn_cotangent.reshape(clip_count, frame_dev, positions, model_width),
        ],
        axis=3,
    )
    both = lax.all_to_all(both, "frame", split_axis=2, concat_axis=1, tiled=True)
    frames = both.shape[1]
    across = both.shape[2]
    values_in = both[:, :, :, 0].astype(jnp.float32)
    average = jnp.mean(values_in, axis=-1, keepdims=True)
    centered = values_in - average
    variance = jnp.mean(centered * centered, axis=-1, keepdims=True)
    inverse_std = lax.rsqrt(variance + 1e-06)
    normed = centered * inverse_std
    modulation = modulation_table[timestep].astype(jnp.float32)
    shift = modulation[:, 0][:, None, None, :]
    scale = modulation[:, 1][:, None, None, :]
    modulated = (normed * (1.0 + scale) + shift).astype(jnp.bfloat16)
    mod_rows = modulated.reshape(-1, model_width)
    projected = jnp.dot(mod_rows, w_full, preferred_element_type=jnp.float32).astype(jnp.bfloat16)
    pieces = projected.reshape(clip_count, frames, across, 3, HEADS, HEAD_DIM)
    loss_weight = snr_table[weight_index]
    upstream = (
        loss_weight[:, None, None, None] * both[:, :, :, 1].astype(jnp.float32)
    ).astype(jnp.bfloat16)
    upstream = upstream.reshape(clip_count, frames, across, HEADS, HEAD_DIM)
    head_grads = attend_back(pieces[:, :, :, 0], pieces[:, :, :, 1], pieces[:, :, :, 2], upstream)
    grad_rows = jnp.stack(head_grads, axis=3).reshape(-1, 3 * model_width)
    grad_scale_factor = float(mod_rows.shape[0] * frame_n * space_n) ** (-0.5)
    term = lax.dot_general(
        mod_rows, grad_rows, (((0,), (0,)), ((), ())), preferred_element_type=jnp.float32
    ).astype(jnp.bfloat16)
    term, grad_rows = lax.optimization_barrier((term, grad_rows))
    col_blk = 3 * model_width // frame_n
    share = lax.psum_scatter(term, "space", scatter_dimension=0, tiled=True)
    row_blk = share.shape[0]
    share = share.reshape(row_blk, frame_n, col_blk).transpose(1, 0, 2)
    grad_hidden = lax.dot_general(
        grad_rows, w_full, (((1,), (1,)), ((), ())), preferred_element_type=jnp.float32
    )
    grad_hidden = grad_hidden.reshape(values_in.shape)
    local_sums = jnp.stack(
        [jnp.sum(grad_hidden, axis=(1, 2)), jnp.sum(grad_hidden * normed, axis=(1, 2))],
        axis=1,
    )
    local_sums = local_sums.reshape(-1, model_width)
    gm = reduce_sums(local_sums, frame_n, space_n)
    gw = reduce_weight(share, frame_n).astype(jnp.float32)
    grad_weight = gw.transpose(1, 0, 2).reshape(row_blk, 3 * model_width) * grad_scale_factor
    grad_modulation = gm.reshape(clip_count, 2, model_width) * grad_scale_factor
    grad_normed = grad_hidden * (1.0 + scale)
    grad_input = (
        grad_normed
        - jnp.mean(grad_normed, axis=-1, keepdims=True)
        - normed * jnp.mean(grad_normed * normed, axis=-1, keepdims=True)
    ) * inverse_std
    grad_input = grad_input.astype(jnp.bfloat16)
    grad_input = lax.all_to_all(grad_input, "frame", split_axis=1, concat_axis=2, tiled=True)
    grad_input = grad_input.reshape(clip_count, frame_dev, row_dev, col_count, model_width)
    return (grad_input, grad_weight, grad_modulation)


def solution(mesh):
    in_specs = (
        P(None, "frame", "space", None, None),
        P(None, "frame", "space", None, None),
        P("space", None),
        P(),
        P(),
        P(),
        P(),
    )
    out_specs = (P(None, "frame", "space", None, None), P("space", None), P())
    return jax.shard_map(
        per_device, mesh=mesh, in_specs=in_specs, out_specs=out_specs, check_vma=False
    )
```

```python
import functools

import jax
import jax.numpy as jnp
from jax import lax
from jax.experimental import pallas as pl
from jax.experimental.pallas import tpu as pltpu
from jax.sharding import PartitionSpec as P

MESH = pl.DeviceIdType.MESH

HEADS = 16
HEAD_DIM = 72


def attend_back(queries, keys, values, upstream):
    factor = queries.shape[-1] ** (-0.5)
    f32 = jnp.float32
    high = lax.Precision.HIGH
    scores = jnp.einsum("bfxhe,bgxhe->bxhfg", queries, keys, preferred_element_type=f32) * factor
    expd = jnp.exp(scores)
    probs = expd / jnp.sum(expd, axis=-1, keepdims=True)
    grad_probs = jnp.einsum("bfxhe,bgxhe->bxhfg", upstream, values, preferred_element_type=f32)
    grad_values = jnp.einsum(
        "bxhfg,bfxhe->bgxhe", probs, upstream.astype(f32), precision=high
    )
    grad_scores = probs * (grad_probs - jnp.sum(probs * grad_probs, axis=-1, keepdims=True))
    grad_queries = jnp.einsum(
        "bxhfg,bgxhe->bfxhe", grad_scores, keys.astype(f32), precision=high
    ) * factor
    grad_keys = jnp.einsum(
        "bxhfg,bfxhe->bgxhe", grad_scores, queries.astype(f32), precision=high
    ) * factor
    return (
        grad_queries.astype(jnp.bfloat16),
        grad_keys.astype(jnp.bfloat16),
        grad_values.astype(jnp.bfloat16),
    )


def barrier_with(peers):
    barrier = pltpu.get_barrier_semaphore()
    for p in peers:
        pl.semaphore_signal(barrier, inc=1, device_id=p, device_id_type=MESH)
    pl.semaphore_wait(barrier, len(peers))


def exchange(src_ref, dst, peer_of, index_of, count, send_sem, recv_sem):
    sends = []
    for k in range(1, count):
        t = lax.rem(index_of + k, count)
        c = pltpu.make_async_remote_copy(
            src_ref=src_ref(t), dst_ref=dst.at[index_of], send_sem=send_sem.at[k],
            recv_sem=recv_sem.at[index_of], device_id=peer_of(t), device_id_type=MESH,
        )
        c.start()
        sends.append(c)
    return sends


def wait_all(src_ref, dst, peer_of, index_of, count, send_sem, recv_sem, sends):
    for k in range(1, count):
        src = lax.rem(index_of + count - k, count)
        pltpu.make_async_remote_copy(
            src_ref=src_ref(0), dst_ref=dst.at[src], send_sem=send_sem.at[k],
            recv_sem=recv_sem.at[src], device_id=peer_of(src), device_id_type=MESH,
        ).wait_recv()
    for c in sends:
        c.wait_send()


def space_parts(sub, s):
    nz, nx, nc = sub
    return (s // (nx * nc), lax.rem(s // nc, nx), lax.rem(s, nc))


def space_index(sub):
    nz, nx, nc = sub
    return (lax.axis_index("sz") * nx + lax.axis_index("sx")) * nc + lax.axis_index("sc")


def weight_kernel(nf, sub, chunks_ref, gw_ref, recv1, redbuf, recv2, s1, r1, s2, r2):
    me_f = lax.axis_index("frame")
    here = space_parts(sub, space_index(sub))
    peer = lambda t: (t,) + here
    barrier_with([peer(lax.rem(me_f + k, nf)) for k in range(1, nf)])
    first = lambda t: chunks_ref.at[t]
    sends = exchange(first, recv1, peer, me_f, nf, s1, r1)
    recv1[me_f] = chunks_ref[me_f]
    wait_all(first, recv1, peer, me_f, nf, s1, r1, sends)
    acc = recv1[0].astype(jnp.float32)
    for j in range(1, nf):
        acc = acc + recv1[j].astype(jnp.float32)
    acc = acc.astype(redbuf.dtype)
    redbuf[...] = acc
    recv2[me_f] = acc
    second = lambda t: redbuf
    sends = exchange(second, recv2, peer, me_f, nf, s2, r2)
    wait_all(second, recv2, peer, me_f, nf, s2, r2, sends)
    gw_ref[...] = recv2[...]


def sums_kernel(nf, sub, sums_ref, gm_ref, msum1, mbuf, msum2, s1, r1, s2, r2):
    ns = sub[0] * sub[1] * sub[2]
    me_f = lax.axis_index("frame")
    me_s = space_index(sub)
    fpeer = lambda t: (t,) + space_parts(sub, me_s)
    speer = lambda t: (me_f,) + space_parts(sub, t)
    barrier_with(
        [fpeer(lax.rem(me_f + k, nf)) for k in range(1, nf)]
        + [speer(lax.rem(me_s + k, ns)) for k in range(1, ns)]
    )
    first = lambda t: sums_ref
    sends = exchange(first, msum1, fpeer, me_f, nf, s1, r1)
    msum1[me_f] = sums_ref[...]
    wait_all(first, msum1, fpeer, me_f, nf, s1, r1, sends)
    macc = msum1[0]
    for j in range(1, nf):
        macc = macc + msum1[j]
    mbuf[...] = macc
    msum2[me_s] = macc
    second = lambda t: mbuf
    sends = exchange(second, msum2, speer, me_s, ns, s2, r2)
    wait_all(second, msum2, speer, me_s, ns, s2, r2, sends)
    total = msum2[0]
    for j in range(1, ns):
        total = total + msum2[j]
    gm_ref[...] = total


def reduce_weight(chunks, nf, sub):
    count, rows, cols = chunks.shape
    vmem = pl.BlockSpec(memory_space=pltpu.VMEM)
    return pl.pallas_call(
        functools.partial(weight_kernel, nf, sub),
        out_shape=jax.ShapeDtypeStruct((count, rows, cols), chunks.dtype),
        in_specs=[vmem],
        out_specs=vmem,
        scratch_shapes=[
            pltpu.VMEM((nf, rows, cols), chunks.dtype),
            pltpu.VMEM((rows, cols), chunks.dtype),
            pltpu.VMEM((nf, rows, cols), chunks.dtype),
        ]
        + [pltpu.SemaphoreType.DMA((nf,))] * 4,
        compiler_params=pltpu.CompilerParams(collective_id=0, has_side_effects=True),
    )(chunks)


def reduce_sums(sums, nf, sub):
    ns = sub[0] * sub[1] * sub[2]
    vmem = pl.BlockSpec(memory_space=pltpu.VMEM)
    return pl.pallas_call(
        functools.partial(sums_kernel, nf, sub),
        out_shape=jax.ShapeDtypeStruct(sums.shape, jnp.float32),
        in_specs=[vmem],
        out_specs=vmem,
        scratch_shapes=[
            pltpu.VMEM((nf,) + sums.shape, jnp.float32),
            pltpu.VMEM(sums.shape, jnp.float32),
            pltpu.VMEM((ns,) + sums.shape, jnp.float32),
        ]
        + [pltpu.SemaphoreType.DMA((nf,)), pltpu.SemaphoreType.DMA((nf,))]
        + [pltpu.SemaphoreType.DMA((ns,)), pltpu.SemaphoreType.DMA((ns,))],
        compiler_params=pltpu.CompilerParams(collective_id=1, has_side_effects=True),
    )(sums)


def per_device(
    hidden_in, attn_cotangent, w_qkv, modulation_table, snr_table, timestep, weight_index
):
    clip_count, frame_dev, row_dev, col_count, model_width = hidden_in.shape
    frame_n = lax.axis_size("frame")
    sub = (lax.axis_size("sz"), lax.axis_size("sx"), lax.axis_size("sc"))
    space_n = sub[0] * sub[1] * sub[2]
    positions = row_dev * col_count
    w_full = lax.all_gather(w_qkv, ("sz", "sx", "sc"), axis=0, tiled=True)
    both = jnp.stack(
        [
            hidden_in.reshape(clip_count, frame_dev, positions, model_width),
            attn_cotangent.reshape(clip_count, frame_dev, positions, model_width),
        ],
        axis=3,
    )
    both = lax.all_to_all(both, "frame", split_axis=2, concat_axis=1, tiled=True)
    frames = both.shape[1]
    across = both.shape[2]
    values_in = both[:, :, :, 0].astype(jnp.float32)
    average = jnp.mean(values_in, axis=-1, keepdims=True)
    centered = values_in - average
    variance = jnp.mean(centered * centered, axis=-1, keepdims=True)
    inverse_std = lax.rsqrt(variance + 1e-06)
    normed = centered * inverse_std
    modulation = modulation_table[timestep].astype(jnp.float32)
    shift = modulation[:, 0][:, None, None, :]
    scale = modulation[:, 1][:, None, None, :]
    modulated = (normed * (1.0 + scale) + shift).astype(jnp.bfloat16)
    mod_rows = modulated.reshape(-1, model_width)
    projected = jnp.dot(mod_rows, w_full, preferred_element_type=jnp.float32).astype(jnp.bfloat16)
    pieces = projected.reshape(clip_count, frames, across, 3, HEADS, HEAD_DIM)
    loss_weight = snr_table[weight_index]
    upstream = (
        loss_weight[:, None, None, None] * both[:, :, :, 1].astype(jnp.float32)
    ).astype(jnp.bfloat16)
    upstream = upstream.reshape(clip_count, frames, across, HEADS, HEAD_DIM)
    head_grads = attend_back(pieces[:, :, :, 0], pieces[:, :, :, 1], pieces[:, :, :, 2], upstream)
    grad_rows = jnp.stack(head_grads, axis=3).reshape(-1, 3 * model_width)
    grad_scale_factor = float(mod_rows.shape[0] * frame_n * space_n) ** (-0.5)
    term = lax.dot_general(
        mod_rows, grad_rows, (((0,), (0,)), ((), ())), preferred_element_type=jnp.float32
    ).astype(jnp.bfloat16)
    term, grad_rows = lax.optimization_barrier((term, grad_rows))
    col_blk = 3 * model_width // frame_n
    nz, nx, nc = sub
    row_blk = model_width // space_n
    share = term.reshape(nz, nx, nc, row_blk, 3 * model_width)
    share = lax.all_to_all(share, "sc", split_axis=2, concat_axis=2, tiled=True)
    share = jnp.sum(share.astype(jnp.float32), axis=2).astype(jnp.bfloat16)
    share = share.reshape(nz * nx, row_blk, 3 * model_width)
    share = lax.all_to_all(share, ("sz", "sx"), split_axis=0, concat_axis=0, tiled=True)
    share = jnp.sum(share.astype(jnp.float32), axis=0).astype(jnp.bfloat16)
    share = share.reshape(row_blk, frame_n, col_blk).transpose(1, 0, 2)
    grad_hidden = lax.dot_general(
        grad_rows, w_full, (((1,), (1,)), ((), ())), preferred_element_type=jnp.float32
    )
    grad_hidden = grad_hidden.reshape(values_in.shape)
    local_sums = jnp.stack(
        [jnp.sum(grad_hidden, axis=(1, 2)), jnp.sum(grad_hidden * normed, axis=(1, 2))],
        axis=1,
    )
    local_sums = local_sums.reshape(-1, model_width)
    gm = reduce_sums(local_sums, frame_n, sub)
    gw = reduce_weight(share, frame_n, sub).astype(jnp.float32)
    grad_weight = gw.transpose(1, 0, 2).reshape(row_blk, 3 * model_width) * grad_scale_factor
    grad_modulation = gm.reshape(clip_count, 2, model_width) * grad_scale_factor
    grad_normed = grad_hidden * (1.0 + scale)
    grad_input = (
        grad_normed
        - jnp.mean(grad_normed, axis=-1, keepdims=True)
        - normed * jnp.mean(grad_normed * normed, axis=-1, keepdims=True)
    ) * inverse_std
    grad_input = grad_input.astype(jnp.bfloat16)
    grad_input = lax.all_to_all(grad_input, "frame", split_axis=1, concat_axis=2, tiled=True)
    grad_input = grad_input.reshape(clip_count, frame_dev, row_dev, col_count, model_width)
    return (grad_input, grad_weight, grad_modulation)


def solution(mesh):
    space_sub = (2, 4, 2)
    devices = mesh.devices.reshape((mesh.shape["frame"],) + space_sub)
    fine = jax.sharding.Mesh(devices, ("frame", "sz", "sx", "sc"))
    space = ("sz", "sx", "sc")
    in_specs = (
        P(None, "frame", space, None, None),
        P(None, "frame", space, None, None),
        P(space, None),
        P(),
        P(),
        P(),
        P(),
    )
    out_specs = (P(None, "frame", space, None, None), P(space, None), P())
    return jax.shard_map(
        per_device, mesh=fine, in_specs=in_specs, out_specs=out_specs, check_vma=False
    )
```

```python
import functools

import jax
import jax.numpy as jnp
from jax import lax
from jax.experimental import pallas as pl
from jax.experimental.pallas import tpu as pltpu
from jax.sharding import PartitionSpec as P

MESH = pl.DeviceIdType.MESH

HEADS = 16
HEAD_DIM = 72


def attend_back(queries, keys, values, upstream):
    factor = queries.shape[-1] ** (-0.5)
    f32 = jnp.float32
    high = lax.Precision.HIGH
    scores = jnp.einsum("bfxhe,bgxhe->bxhfg", queries, keys, preferred_element_type=f32) * factor
    expd = jnp.exp(scores)
    probs = expd / jnp.sum(expd, axis=-1, keepdims=True)
    grad_probs = jnp.einsum("bfxhe,bgxhe->bxhfg", upstream, values, preferred_element_type=f32)
    grad_values = jnp.einsum(
        "bxhfg,bfxhe->bgxhe", probs, upstream.astype(f32), precision=high
    )
    grad_scores = probs * (grad_probs - jnp.sum(probs * grad_probs, axis=-1, keepdims=True))
    grad_queries = jnp.einsum(
        "bxhfg,bgxhe->bfxhe", grad_scores, keys.astype(f32), precision=high
    ) * factor
    grad_keys = jnp.einsum(
        "bxhfg,bfxhe->bgxhe", grad_scores, queries.astype(f32), precision=high
    ) * factor
    return (
        grad_queries.astype(jnp.bfloat16),
        grad_keys.astype(jnp.bfloat16),
        grad_values.astype(jnp.bfloat16),
    )


def barrier_with(peers):
    barrier = pltpu.get_barrier_semaphore()
    for p in peers:
        pl.semaphore_signal(barrier, inc=1, device_id=p, device_id_type=MESH)
    pl.semaphore_wait(barrier, len(peers))


def exchange(src_ref, dst, peer_of, index_of, count, send_sem, recv_sem):
    sends = []
    for k in range(1, count):
        t = lax.rem(index_of + k, count)
        c = pltpu.make_async_remote_copy(
            src_ref=src_ref(t), dst_ref=dst.at[index_of], send_sem=send_sem.at[k],
            recv_sem=recv_sem.at[index_of], device_id=peer_of(t), device_id_type=MESH,
        )
        c.start()
        sends.append(c)
    return sends


def wait_all(src_ref, dst, peer_of, index_of, count, send_sem, recv_sem, sends):
    for k in range(1, count):
        src = lax.rem(index_of + count - k, count)
        pltpu.make_async_remote_copy(
            src_ref=src_ref(0), dst_ref=dst.at[src], send_sem=send_sem.at[k],
            recv_sem=recv_sem.at[src], device_id=peer_of(src), device_id_type=MESH,
        ).wait_recv()
    for c in sends:
        c.wait_send()


def space_parts(sub, s):
    nz, nx, nc = sub
    return (s // (nx * nc), lax.rem(s // nc, nx), lax.rem(s, nc))


def space_index(sub):
    nz, nx, nc = sub
    return (lax.axis_index("sz") * nx + lax.axis_index("sx")) * nc + lax.axis_index("sc")


def weight_kernel(nf, sub, chunks_ref, gw_ref, recv1, redbuf, recv2, s1, r1, s2, r2):
    me_f = lax.axis_index("frame")
    here = space_parts(sub, space_index(sub))
    peer = lambda t: (t,) + here
    barrier_with([peer(lax.rem(me_f + k, nf)) for k in range(1, nf)])
    first = lambda t: chunks_ref.at[t]
    sends = exchange(first, recv1, peer, me_f, nf, s1, r1)
    recv1[me_f] = chunks_ref[me_f]
    wait_all(first, recv1, peer, me_f, nf, s1, r1, sends)
    acc = recv1[0].astype(jnp.float32)
    for j in range(1, nf):
        acc = acc + recv1[j].astype(jnp.float32)
    acc = acc.astype(redbuf.dtype)
    redbuf[...] = acc
    recv2[me_f] = acc
    second = lambda t: redbuf
    sends = exchange(second, recv2, peer, me_f, nf, s2, r2)
    wait_all(second, recv2, peer, me_f, nf, s2, r2, sends)
    gw_ref[...] = recv2[...]


def sums_kernel(nf, sub, sums_ref, gm_ref, msum1, mbuf, msum2, s1, r1, s2, r2):
    ns = sub[0] * sub[1] * sub[2]
    me_f = lax.axis_index("frame")
    me_s = space_index(sub)
    fpeer = lambda t: (t,) + space_parts(sub, me_s)
    speer = lambda t: (me_f,) + space_parts(sub, t)
    barrier_with(
        [fpeer(lax.rem(me_f + k, nf)) for k in range(1, nf)]
        + [speer(lax.rem(me_s + k, ns)) for k in range(1, ns)]
    )
    first = lambda t: sums_ref
    sends = exchange(first, msum1, fpeer, me_f, nf, s1, r1)
    msum1[me_f] = sums_ref[...]
    wait_all(first, msum1, fpeer, me_f, nf, s1, r1, sends)
    macc = msum1[0]
    for j in range(1, nf):
        macc = macc + msum1[j]
    mbuf[...] = macc
    msum2[me_s] = macc
    second = lambda t: mbuf
    sends = exchange(second, msum2, speer, me_s, ns, s2, r2)
    wait_all(second, msum2, speer, me_s, ns, s2, r2, sends)
    total = msum2[0]
    for j in range(1, ns):
        total = total + msum2[j]
    gm_ref[...] = total


def reduce_weight(chunks, nf, sub):
    count, rows, cols = chunks.shape
    vmem = pl.BlockSpec(memory_space=pltpu.VMEM)
    return pl.pallas_call(
        functools.partial(weight_kernel, nf, sub),
        out_shape=jax.ShapeDtypeStruct((count, rows, cols), chunks.dtype),
        in_specs=[vmem],
        out_specs=vmem,
        scratch_shapes=[
            pltpu.VMEM((nf, rows, cols), chunks.dtype),
            pltpu.VMEM((rows, cols), chunks.dtype),
            pltpu.VMEM((nf, rows, cols), chunks.dtype),
        ]
        + [pltpu.SemaphoreType.DMA((nf,))] * 4,
        compiler_params=pltpu.CompilerParams(collective_id=0, has_side_effects=True),
    )(chunks)


def reduce_sums(sums, nf, sub):
    ns = sub[0] * sub[1] * sub[2]
    vmem = pl.BlockSpec(memory_space=pltpu.VMEM)
    return pl.pallas_call(
        functools.partial(sums_kernel, nf, sub),
        out_shape=jax.ShapeDtypeStruct(sums.shape, jnp.float32),
        in_specs=[vmem],
        out_specs=vmem,
        scratch_shapes=[
            pltpu.VMEM((nf,) + sums.shape, jnp.float32),
            pltpu.VMEM(sums.shape, jnp.float32),
            pltpu.VMEM((ns,) + sums.shape, jnp.float32),
        ]
        + [pltpu.SemaphoreType.DMA((nf,)), pltpu.SemaphoreType.DMA((nf,))]
        + [pltpu.SemaphoreType.DMA((ns,)), pltpu.SemaphoreType.DMA((ns,))],
        compiler_params=pltpu.CompilerParams(collective_id=1, has_side_effects=True),
    )(sums)


def per_device(
    hidden_in, attn_cotangent, w_qkv, modulation_table, snr_table, timestep, weight_index
):
    clip_count, frame_dev, row_dev, col_count, model_width = hidden_in.shape
    frame_n = lax.axis_size("frame")
    sub = (lax.axis_size("sz"), lax.axis_size("sx"), lax.axis_size("sc"))
    space_n = sub[0] * sub[1] * sub[2]
    positions = row_dev * col_count
    w_full = lax.all_gather(w_qkv, ("sz", "sx"), axis=0)
    w_full = jnp.broadcast_to(w_full[:, None], (sub[0] * sub[1], sub[2]) + w_qkv.shape)
    w_full = lax.all_to_all(w_full, "sc", split_axis=1, concat_axis=1, tiled=True)
    w_full = w_full.reshape(-1, w_qkv.shape[1])
    both = jnp.stack(
        [
            hidden_in.reshape(clip_count, frame_dev, positions, model_width),
            attn_cotangent.reshape(clip_count, frame_dev, positions, model_width),
        ],
        axis=3,
    )
    both = lax.all_to_all(both, "frame", split_axis=2, concat_axis=1, tiled=True)
    frames = both.shape[1]
    across = both.shape[2]
    values_in = both[:, :, :, 0].astype(jnp.float32)
    average = jnp.mean(values_in, axis=-1, keepdims=True)
    centered = values_in - average
    variance = jnp.mean(centered * centered, axis=-1, keepdims=True)
    inverse_std = lax.rsqrt(variance + 1e-06)
    normed = centered * inverse_std
    modulation = modulation_table[timestep].astype(jnp.float32)
    shift = modulation[:, 0][:, None, None, :]
    scale = modulation[:, 1][:, None, None, :]
    modulated = (normed * (1.0 + scale) + shift).astype(jnp.bfloat16)
    mod_rows = modulated.reshape(-1, model_width)
    projected = jnp.dot(mod_rows, w_full, preferred_element_type=jnp.float32).astype(jnp.bfloat16)
    pieces = projected.reshape(clip_count, frames, across, 3, HEADS, HEAD_DIM)
    loss_weight = snr_table[weight_index]
    upstream = (
        loss_weight[:, None, None, None] * both[:, :, :, 1].astype(jnp.float32)
    ).astype(jnp.bfloat16)
    upstream = upstream.reshape(clip_count, frames, across, HEADS, HEAD_DIM)
    head_grads = attend_back(pieces[:, :, :, 0], pieces[:, :, :, 1], pieces[:, :, :, 2], upstream)
    grad_rows = jnp.stack(head_grads, axis=3).reshape(-1, 3 * model_width)
    grad_scale_factor = float(mod_rows.shape[0] * frame_n * space_n) ** (-0.5)
    term = lax.dot_general(
        mod_rows, grad_rows, (((0,), (0,)), ((), ())), preferred_element_type=jnp.float32
    ).astype(jnp.bfloat16)
    term, grad_rows = lax.optimization_barrier((term, grad_rows))
    col_blk = 3 * model_width // frame_n
    share = lax.psum_scatter(term, ("sz", "sx", "sc"), scatter_dimension=0, tiled=True)
    row_blk = share.shape[0]
    share = share.reshape(row_blk, frame_n, col_blk).transpose(1, 0, 2)
    grad_hidden = lax.dot_general(
        grad_rows, w_full, (((1,), (1,)), ((), ())), preferred_element_type=jnp.float32
    )
    grad_hidden = grad_hidden.reshape(values_in.shape)
    local_sums = jnp.stack(
        [jnp.sum(grad_hidden, axis=(1, 2)), jnp.sum(grad_hidden * normed, axis=(1, 2))],
        axis=1,
    )
    local_sums = local_sums.reshape(-1, model_width)
    gm = reduce_sums(local_sums, frame_n, sub)
    gw = reduce_weight(share, frame_n, sub).astype(jnp.float32)
    grad_weight = gw.transpose(1, 0, 2).reshape(row_blk, 3 * model_width) * grad_scale_factor
    grad_modulation = gm.reshape(clip_count, 2, model_width) * grad_scale_factor
    grad_normed = grad_hidden * (1.0 + scale)
    grad_input = (
        grad_normed
        - jnp.mean(grad_normed, axis=-1, keepdims=True)
        - normed * jnp.mean(grad_normed * normed, axis=-1, keepdims=True)
    ) * inverse_std
    grad_input = grad_input.astype(jnp.bfloat16)
    grad_input = lax.all_to_all(grad_input, "frame", split_axis=1, concat_axis=2, tiled=True)
    grad_input = grad_input.reshape(clip_count, frame_dev, row_dev, col_count, model_width)
    return (grad_input, grad_weight, grad_modulation)


def solution(mesh):
    space_sub = (2, 4, 2)
    devices = mesh.devices.reshape((mesh.shape["frame"],) + space_sub)
    fine = jax.sharding.Mesh(devices, ("frame", "sz", "sx", "sc"))
    space = ("sz", "sx", "sc")
    in_specs = (
        P(None, "frame", space, None, None),
        P(None, "frame", space, None, None),
        P(space, None),
        P(),
        P(),
        P(),
        P(),
    )
    out_specs = (P(None, "frame", space, None, None), P(space, None), P())
    return jax.shard_map(
        per_device, mesh=fine, in_specs=in_specs, out_specs=out_specs, check_vma=False
    )
```

```python
import functools

import jax
import jax.numpy as jnp
from jax import lax
from jax.experimental import pallas as pl
from jax.experimental.pallas import tpu as pltpu
from jax.sharding import PartitionSpec as P

MESH = pl.DeviceIdType.MESH

HEADS = 16
HEAD_DIM = 72


def attend_back(queries, keys, values, upstream):
    factor = queries.shape[-1] ** (-0.5)
    f32 = jnp.float32
    high = lax.Precision.HIGH
    scores = jnp.einsum("bfxhe,bgxhe->bxhfg", queries, keys, preferred_element_type=f32) * factor
    expd = jnp.exp(scores)
    probs = expd / jnp.sum(expd, axis=-1, keepdims=True)
    grad_probs = jnp.einsum("bfxhe,bgxhe->bxhfg", upstream, values, preferred_element_type=f32)
    grad_values = jnp.einsum(
        "bxhfg,bfxhe->bgxhe", probs, upstream.astype(f32), precision=high
    )
    grad_scores = probs * (grad_probs - jnp.sum(probs * grad_probs, axis=-1, keepdims=True))
    grad_queries = jnp.einsum(
        "bxhfg,bgxhe->bfxhe", grad_scores, keys.astype(f32), precision=high
    ) * factor
    grad_keys = jnp.einsum(
        "bxhfg,bfxhe->bgxhe", grad_scores, queries.astype(f32), precision=high
    ) * factor
    return (
        grad_queries.astype(jnp.bfloat16),
        grad_keys.astype(jnp.bfloat16),
        grad_values.astype(jnp.bfloat16),
    )


def barrier_with(peers):
    barrier = pltpu.get_barrier_semaphore()
    for p in peers:
        pl.semaphore_signal(barrier, inc=1, device_id=p, device_id_type=MESH)
    pl.semaphore_wait(barrier, len(peers))


def exchange(src_ref, dst, peer_of, index_of, count, send_sem, recv_sem):
    sends = []
    for k in range(1, count):
        t = lax.rem(index_of + k, count)
        c = pltpu.make_async_remote_copy(
            src_ref=src_ref(t), dst_ref=dst.at[index_of], send_sem=send_sem.at[k],
            recv_sem=recv_sem.at[index_of], device_id=peer_of(t), device_id_type=MESH,
        )
        c.start()
        sends.append(c)
    return sends


def wait_all(src_ref, dst, peer_of, index_of, count, send_sem, recv_sem, sends):
    for k in range(1, count):
        src = lax.rem(index_of + count - k, count)
        pltpu.make_async_remote_copy(
            src_ref=src_ref(0), dst_ref=dst.at[src], send_sem=send_sem.at[k],
            recv_sem=recv_sem.at[src], device_id=peer_of(src), device_id_type=MESH,
        ).wait_recv()
    for c in sends:
        c.wait_send()


def weight_kernel(nf, scale, share_ref, gw_ref, chunks, recv1, redbuf, recv2, s1, r1, s2, r2):
    cols = chunks.shape[2]
    for j in range(nf):
        chunks[j] = share_ref[:, j * cols:(j + 1) * cols]
    me_f = lax.axis_index("frame")
    me_s = lax.axis_index("space")
    peer = lambda t: (t, me_s)
    barrier_with([peer(lax.rem(me_f + k, nf)) for k in range(1, nf)])
    first = lambda t: chunks.at[t]
    sends = exchange(first, recv1, peer, me_f, nf, s1, r1)
    recv1[me_f] = chunks[me_f]
    wait_all(first, recv1, peer, me_f, nf, s1, r1, sends)
    acc = recv1[0].astype(jnp.float32)
    for j in range(1, nf):
        acc = acc + recv1[j].astype(jnp.float32)
    acc = acc.astype(redbuf.dtype)
    redbuf[...] = acc
    recv2[me_f] = acc
    second = lambda t: redbuf
    sends = exchange(second, recv2, peer, me_f, nf, s2, r2)
    wait_all(second, recv2, peer, me_f, nf, s2, r2, sends)
    for j in range(nf):
        gw_ref[:, j * cols:(j + 1) * cols] = recv2[j].astype(jnp.float32) * scale


def sums_kernel(nf, ns, sums_ref, gm_ref, msum1, mbuf, msum2, s1, r1, s2, r2):
    me_f = lax.axis_index("frame")
    me_s = lax.axis_index("space")
    fpeer = lambda t: (t, me_s)
    speer = lambda t: (me_f, t)
    barrier_with(
        [fpeer(lax.rem(me_f + k, nf)) for k in range(1, nf)]
        + [speer(lax.rem(me_s + k, ns)) for k in range(1, ns)]
    )
    first = lambda t: sums_ref
    sends = exchange(first, msum1, fpeer, me_f, nf, s1, r1)
    msum1[me_f] = sums_ref[...]
    wait_all(first, msum1, fpeer, me_f, nf, s1, r1, sends)
    macc = msum1[0]
    for j in range(1, nf):
        macc = macc + msum1[j]
    mbuf[...] = macc
    msum2[me_s] = macc
    second = lambda t: mbuf
    sends = exchange(second, msum2, speer, me_s, ns, s2, r2)
    wait_all(second, msum2, speer, me_s, ns, s2, r2, sends)
    total = msum2[0]
    for j in range(1, ns):
        total = total + msum2[j]
    gm_ref[...] = total


def reduce_weight(share, nf, scale):
    rows, width = share.shape
    cols = width // nf
    vmem = pl.BlockSpec(memory_space=pltpu.VMEM)
    return pl.pallas_call(
        functools.partial(weight_kernel, nf, scale),
        out_shape=jax.ShapeDtypeStruct((rows, width), jnp.float32),
        in_specs=[vmem],
        out_specs=vmem,
        scratch_shapes=[
            pltpu.VMEM((nf, rows, cols), share.dtype),
            pltpu.VMEM((nf, rows, cols), share.dtype),
            pltpu.VMEM((rows, cols), share.dtype),
            pltpu.VMEM((nf, rows, cols), share.dtype),
        ]
        + [pltpu.SemaphoreType.DMA((nf,))] * 4,
        compiler_params=pltpu.CompilerParams(collective_id=0, has_side_effects=True),
    )(share)


def reduce_sums(sums, nf, ns):
    vmem = pl.BlockSpec(memory_space=pltpu.VMEM)
    return pl.pallas_call(
        functools.partial(sums_kernel, nf, ns),
        out_shape=jax.ShapeDtypeStruct(sums.shape, jnp.float32),
        in_specs=[vmem],
        out_specs=vmem,
        scratch_shapes=[
            pltpu.VMEM((nf,) + sums.shape, jnp.float32),
            pltpu.VMEM(sums.shape, jnp.float32),
            pltpu.VMEM((ns,) + sums.shape, jnp.float32),
        ]
        + [pltpu.SemaphoreType.DMA((nf,)), pltpu.SemaphoreType.DMA((nf,))]
        + [pltpu.SemaphoreType.DMA((ns,)), pltpu.SemaphoreType.DMA((ns,))],
        compiler_params=pltpu.CompilerParams(collective_id=1, has_side_effects=True),
    )(sums)


def per_device(
    hidden_in, attn_cotangent, w_qkv, modulation_table, snr_table, timestep, weight_index
):
    clip_count, frame_dev, row_dev, col_count, model_width = hidden_in.shape
    frame_n = lax.axis_size("frame")
    space_n = lax.axis_size("space")
    positions = row_dev * col_count
    w_full = lax.all_gather(w_qkv, "space", axis=0, tiled=True)
    both = jnp.stack(
        [
            hidden_in.reshape(clip_count, frame_dev, positions, model_width),
            attn_cotangent.reshape(clip_count, frame_dev, positions, model_width),
        ],
        axis=3,
    )
    both = lax.all_to_all(both, "frame", split_axis=2, concat_axis=1, tiled=True)
    frames = both.shape[1]
    across = both.shape[2]
    values_in = both[:, :, :, 0].astype(jnp.float32)
    average = jnp.mean(values_in, axis=-1, keepdims=True)
    centered = values_in - average
    variance = jnp.mean(centered * centered, axis=-1, keepdims=True)
    inverse_std = lax.rsqrt(variance + 1e-06)
    normed = centered * inverse_std
    modulation = modulation_table[timestep].astype(jnp.float32)
    shift = modulation[:, 0][:, None, None, :]
    scale = modulation[:, 1][:, None, None, :]
    modulated = (normed * (1.0 + scale) + shift).astype(jnp.bfloat16)
    mod_rows = modulated.reshape(-1, model_width)
    projected = jnp.dot(mod_rows, w_full, preferred_element_type=jnp.float32).astype(jnp.bfloat16)
    pieces = projected.reshape(clip_count, frames, across, 3, HEADS, HEAD_DIM)
    loss_weight = snr_table[weight_index]
    upstream = (
        loss_weight[:, None, None, None] * both[:, :, :, 1].astype(jnp.float32)
    ).astype(jnp.bfloat16)
    upstream = upstream.reshape(clip_count, frames, across, HEADS, HEAD_DIM)
    head_grads = attend_back(pieces[:, :, :, 0], pieces[:, :, :, 1], pieces[:, :, :, 2], upstream)
    grad_rows = jnp.stack(head_grads, axis=3).reshape(-1, 3 * model_width)
    grad_scale_factor = float(mod_rows.shape[0] * frame_n * space_n) ** (-0.5)
    term = lax.dot_general(
        mod_rows, grad_rows, (((0,), (0,)), ((), ())), preferred_element_type=jnp.float32
    ).astype(jnp.bfloat16)
    term, grad_rows = lax.optimization_barrier((term, grad_rows))
    col_blk = 3 * model_width // frame_n
    share = lax.psum_scatter(term, "space", scatter_dimension=0, tiled=True)
    grad_hidden = lax.dot_general(
        grad_rows, w_full, (((1,), (1,)), ((), ())), preferred_element_type=jnp.float32
    )
    grad_hidden = grad_hidden.reshape(values_in.shape)
    local_sums = jnp.stack(
        [jnp.sum(grad_hidden, axis=(1, 2)), jnp.sum(grad_hidden * normed, axis=(1, 2))],
        axis=1,
    )
    local_sums = local_sums.reshape(-1, model_width)
    gm = reduce_sums(local_sums, frame_n, space_n)
    grad_weight = reduce_weight(share, frame_n, grad_scale_factor)
    grad_modulation = gm.reshape(clip_count, 2, model_width) * grad_scale_factor
    grad_normed = grad_hidden * (1.0 + scale)
    grad_input = (
        grad_normed
        - jnp.mean(grad_normed, axis=-1, keepdims=True)
        - normed * jnp.mean(grad_normed * normed, axis=-1, keepdims=True)
    ) * inverse_std
    grad_input = grad_input.astype(jnp.bfloat16)
    grad_input = lax.all_to_all(grad_input, "frame", split_axis=1, concat_axis=2, tiled=True)
    grad_input = grad_input.reshape(clip_count, frame_dev, row_dev, col_count, model_width)
    return (grad_input, grad_weight, grad_modulation)


def solution(mesh):
    in_specs = (
        P(None, "frame", "space", None, None),
        P(None, "frame", "space", None, None),
        P("space", None),
        P(),
        P(),
        P(),
        P(),
    )
    out_specs = (P(None, "frame", "space", None, None), P("space", None), P())
    return jax.shard_map(
        per_device, mesh=mesh, in_specs=in_specs, out_specs=out_specs, check_vma=False
    )
```

```python
import functools

import jax
import jax.numpy as jnp
from jax import lax
from jax.experimental import pallas as pl
from jax.experimental.pallas import tpu as pltpu
from jax.sharding import PartitionSpec as P

MESH = pl.DeviceIdType.MESH

HEADS = 16
HEAD_DIM = 72


def attend_back(queries, keys, values, upstream):
    factor = queries.shape[-1] ** (-0.5)
    f32 = jnp.float32
    high = lax.Precision.HIGH
    scores = jnp.einsum("bfxhe,bgxhe->bxhfg", queries, keys, preferred_element_type=f32) * factor
    expd = jnp.exp(scores)
    probs = expd / jnp.sum(expd, axis=-1, keepdims=True)
    grad_probs = jnp.einsum("bfxhe,bgxhe->bxhfg", upstream, values, preferred_element_type=f32)
    grad_values = jnp.einsum(
        "bxhfg,bfxhe->bgxhe", probs, upstream.astype(f32), precision=high
    )
    grad_scores = probs * (grad_probs - jnp.sum(probs * grad_probs, axis=-1, keepdims=True))
    grad_queries = jnp.einsum(
        "bxhfg,bgxhe->bfxhe", grad_scores, keys.astype(f32), precision=high
    ) * factor
    grad_keys = jnp.einsum(
        "bxhfg,bfxhe->bgxhe", grad_scores, queries.astype(f32), precision=high
    ) * factor
    return (
        grad_queries.astype(jnp.bfloat16),
        grad_keys.astype(jnp.bfloat16),
        grad_values.astype(jnp.bfloat16),
    )


def barrier_with(peers):
    barrier = pltpu.get_barrier_semaphore()
    for p in peers:
        pl.semaphore_signal(barrier, inc=1, device_id=p, device_id_type=MESH)
    pl.semaphore_wait(barrier, len(peers))


def exchange(src_ref, dst, peer_of, index_of, count, send_sem, recv_sem):
    sends = []
    for k in range(1, count):
        t = lax.rem(index_of + k, count)
        c = pltpu.make_async_remote_copy(
            src_ref=src_ref(t), dst_ref=dst.at[index_of], send_sem=send_sem.at[k],
            recv_sem=recv_sem.at[index_of], device_id=peer_of(t), device_id_type=MESH,
        )
        c.start()
        sends.append(c)
    return sends


def wait_all(src_ref, dst, peer_of, index_of, count, send_sem, recv_sem, sends):
    for k in range(1, count):
        src = lax.rem(index_of + count - k, count)
        pltpu.make_async_remote_copy(
            src_ref=src_ref(0), dst_ref=dst.at[src], send_sem=send_sem.at[k],
            recv_sem=recv_sem.at[src], device_id=peer_of(src), device_id_type=MESH,
        ).wait_recv()
    for c in sends:
        c.wait_send()


def weight_kernel(nf, scale, share_ref, gw_ref, chunks, recv1, redbuf, recv2, s1, r1, s2, r2):
    cols = chunks.shape[2]
    me_f = lax.axis_index("frame")
    me_s = lax.axis_index("space")
    peer = lambda t: (t, me_s)
    barrier = pltpu.get_barrier_semaphore()
    for k in range(1, nf):
        pl.semaphore_signal(
            barrier, inc=1, device_id=peer(lax.rem(me_f + k, nf)), device_id_type=MESH
        )
    for j in range(nf):
        chunks[j] = share_ref[:, j * cols:(j + 1) * cols]
    pl.semaphore_wait(barrier, nf - 1)
    first = lambda t: chunks.at[t]
    sends = exchange(first, recv1, peer, me_f, nf, s1, r1)
    recv1[me_f] = chunks[me_f]
    wait_all(first, recv1, peer, me_f, nf, s1, r1, sends)
    acc = recv1[0].astype(jnp.float32)
    for j in range(1, nf):
        acc = acc + recv1[j].astype(jnp.float32)
    acc = acc.astype(redbuf.dtype)
    redbuf[...] = acc
    recv2[me_f] = acc
    second = lambda t: redbuf
    sends = exchange(second, recv2, peer, me_f, nf, s2, r2)
    wait_all(second, recv2, peer, me_f, nf, s2, r2, sends)
    for j in range(nf):
        gw_ref[:, j * cols:(j + 1) * cols] = recv2[j].astype(jnp.float32) * scale


def sums_kernel(nf, ns, sums_ref, gm_ref, msum1, mbuf, msum2, s1, r1, s2, r2):
    me_f = lax.axis_index("frame")
    me_s = lax.axis_index("space")
    fpeer = lambda t: (t, me_s)
    speer = lambda t: (me_f, t)
    barrier_with(
        [fpeer(lax.rem(me_f + k, nf)) for k in range(1, nf)]
        + [speer(lax.rem(me_s + k, ns)) for k in range(1, ns)]
    )
    first = lambda t: sums_ref
    sends = exchange(first, msum1, fpeer, me_f, nf, s1, r1)
    msum1[me_f] = sums_ref[...]
    wait_all(first, msum1, fpeer, me_f, nf, s1, r1, sends)
    macc = msum1[0]
    for j in range(1, nf):
        macc = macc + msum1[j]
    mbuf[...] = macc
    msum2[me_s] = macc
    second = lambda t: mbuf
    sends = exchange(second, msum2, speer, me_s, ns, s2, r2)
    wait_all(second, msum2, speer, me_s, ns, s2, r2, sends)
    total = msum2[0]
    for j in range(1, ns):
        total = total + msum2[j]
    gm_ref[...] = total


def reduce_weight(share, nf, scale):
    rows, width = share.shape
    cols = width // nf
    vmem = pl.BlockSpec(memory_space=pltpu.VMEM)
    return pl.pallas_call(
        functools.partial(weight_kernel, nf, scale),
        out_shape=jax.ShapeDtypeStruct((rows, width), jnp.float32),
        in_specs=[vmem],
        out_specs=vmem,
        scratch_shapes=[
            pltpu.VMEM((nf, rows, cols), share.dtype),
            pltpu.VMEM((nf, rows, cols), share.dtype),
            pltpu.VMEM((rows, cols), share.dtype),
            pltpu.VMEM((nf, rows, cols), share.dtype),
        ]
        + [pltpu.SemaphoreType.DMA((nf,))] * 4,
        compiler_params=pltpu.CompilerParams(collective_id=0, has_side_effects=True),
    )(share)


def reduce_sums(sums, nf, ns):
    vmem = pl.BlockSpec(memory_space=pltpu.VMEM)
    return pl.pallas_call(
        functools.partial(sums_kernel, nf, ns),
        out_shape=jax.ShapeDtypeStruct(sums.shape, jnp.float32),
        in_specs=[vmem],
        out_specs=vmem,
        scratch_shapes=[
            pltpu.VMEM((nf,) + sums.shape, jnp.float32),
            pltpu.VMEM(sums.shape, jnp.float32),
            pltpu.VMEM((ns,) + sums.shape, jnp.float32),
        ]
        + [pltpu.SemaphoreType.DMA((nf,)), pltpu.SemaphoreType.DMA((nf,))]
        + [pltpu.SemaphoreType.DMA((ns,)), pltpu.SemaphoreType.DMA((ns,))],
        compiler_params=pltpu.CompilerParams(collective_id=1, has_side_effects=True),
    )(sums)


def per_device(
    hidden_in, attn_cotangent, w_qkv, modulation_table, snr_table, timestep, weight_index
):
    clip_count, frame_dev, row_dev, col_count, model_width = hidden_in.shape
    frame_n = lax.axis_size("frame")
    space_n = lax.axis_size("space")
    positions = row_dev * col_count
    w_full = lax.all_gather(w_qkv, "space", axis=0, tiled=True)
    both = jnp.stack(
        [
            hidden_in.reshape(clip_count, frame_dev, positions, model_width),
            attn_cotangent.reshape(clip_count, frame_dev, positions, model_width),
        ],
        axis=3,
    )
    both = lax.all_to_all(both, "frame", split_axis=2, concat_axis=1, tiled=True)
    frames = both.shape[1]
    across = both.shape[2]
    values_in = both[:, :, :, 0].astype(jnp.float32)
    average = jnp.mean(values_in, axis=-1, keepdims=True)
    centered = values_in - average
    variance = jnp.mean(centered * centered, axis=-1, keepdims=True)
    inverse_std = lax.rsqrt(variance + 1e-06)
    normed = centered * inverse_std
    modulation = modulation_table[timestep].astype(jnp.float32)
    shift = modulation[:, 0][:, None, None, :]
    scale = modulation[:, 1][:, None, None, :]
    modulated = (normed * (1.0 + scale) + shift).astype(jnp.bfloat16)
    mod_rows = modulated.reshape(-1, model_width)
    projected = jnp.dot(mod_rows, w_full, preferred_element_type=jnp.float32).astype(jnp.bfloat16)
    pieces = projected.reshape(clip_count, frames, across, 3, HEADS, HEAD_DIM)
    loss_weight = snr_table[weight_index]
    upstream = (
        loss_weight[:, None, None, None] * both[:, :, :, 1].astype(jnp.float32)
    ).astype(jnp.bfloat16)
    upstream = upstream.reshape(clip_count, frames, across, HEADS, HEAD_DIM)
    head_grads = attend_back(pieces[:, :, :, 0], pieces[:, :, :, 1], pieces[:, :, :, 2], upstream)
    grad_rows = jnp.stack(head_grads, axis=3).reshape(-1, 3 * model_width)
    grad_scale_factor = float(mod_rows.shape[0] * frame_n * space_n) ** (-0.5)
    term = lax.dot_general(
        mod_rows, grad_rows, (((0,), (0,)), ((), ())), preferred_element_type=jnp.float32
    ).astype(jnp.bfloat16)
    term, grad_rows = lax.optimization_barrier((term, grad_rows))
    col_blk = 3 * model_width // frame_n
    share = lax.psum_scatter(term, "space", scatter_dimension=0, tiled=True)
    grad_hidden = lax.dot_general(
        grad_rows, w_full, (((1,), (1,)), ((), ())), preferred_element_type=jnp.float32
    )
    grad_hidden = grad_hidden.reshape(values_in.shape)
    local_sums = jnp.stack(
        [jnp.sum(grad_hidden, axis=(1, 2)), jnp.sum(grad_hidden * normed, axis=(1, 2))],
        axis=1,
    )
    local_sums = local_sums.reshape(-1, model_width)
    gm = reduce_sums(local_sums, frame_n, space_n)
    grad_weight = reduce_weight(share, frame_n, grad_scale_factor)
    grad_modulation = gm.reshape(clip_count, 2, model_width) * grad_scale_factor
    grad_normed = grad_hidden * (1.0 + scale)
    grad_input = (
        grad_normed
        - jnp.mean(grad_normed, axis=-1, keepdims=True)
        - normed * jnp.mean(grad_normed * normed, axis=-1, keepdims=True)
    ) * inverse_std
    grad_input = grad_input.astype(jnp.bfloat16)
    grad_input = lax.all_to_all(grad_input, "frame", split_axis=1, concat_axis=2, tiled=True)
    grad_input = grad_input.reshape(clip_count, frame_dev, row_dev, col_count, model_width)
    return (grad_input, grad_weight, grad_modulation)


def solution(mesh):
    in_specs = (
        P(None, "frame", "space", None, None),
        P(None, "frame", "space", None, None),
        P("space", None),
        P(),
        P(),
        P(),
        P(),
    )
    out_specs = (P(None, "frame", "space", None, None), P("space", None), P())
    return jax.shard_map(
        per_device, mesh=mesh, in_specs=in_specs, out_specs=out_specs, check_vma=False
    )
```

```python
import functools

import jax
import jax.numpy as jnp
from jax import lax
from jax.experimental import pallas as pl
from jax.experimental.pallas import tpu as pltpu
from jax.sharding import PartitionSpec as P

MESH = pl.DeviceIdType.MESH

HEADS = 16
HEAD_DIM = 72


def attend_back(queries, keys, values, upstream):
    factor = queries.shape[-1] ** (-0.5)
    f32 = jnp.float32
    scores = jnp.einsum("bfxhe,bgxhe->bxhfg", queries, keys, preferred_element_type=f32) * factor
    expd = jnp.exp(scores)
    probs = expd / jnp.sum(expd, axis=-1, keepdims=True)
    grad_probs = jnp.einsum("bfxhe,bgxhe->bxhfg", upstream, values, preferred_element_type=f32)
    def two_pass(spec, factor, operand):
        hi = factor.astype(jnp.bfloat16)
        lo = (factor - hi.astype(f32)).astype(jnp.bfloat16)
        return jnp.einsum(spec, hi, operand, preferred_element_type=f32) + jnp.einsum(
            spec, lo, operand, preferred_element_type=f32
        )

    grad_values = two_pass("bxhfg,bfxhe->bgxhe", probs, upstream)
    grad_scores = probs * (grad_probs - jnp.sum(probs * grad_probs, axis=-1, keepdims=True))
    grad_queries = two_pass("bxhfg,bgxhe->bfxhe", grad_scores, keys) * factor
    grad_keys = two_pass("bxhfg,bfxhe->bgxhe", grad_scores, queries) * factor
    return (
        grad_queries.astype(jnp.bfloat16),
        grad_keys.astype(jnp.bfloat16),
        grad_values.astype(jnp.bfloat16),
    )


def barrier_with(peers):
    barrier = pltpu.get_barrier_semaphore()
    for p in peers:
        pl.semaphore_signal(barrier, inc=1, device_id=p, device_id_type=MESH)
    pl.semaphore_wait(barrier, len(peers))


def exchange(src_ref, dst, peer_of, index_of, count, send_sem, recv_sem):
    sends = []
    for k in range(1, count):
        t = lax.rem(index_of + k, count)
        c = pltpu.make_async_remote_copy(
            src_ref=src_ref(t), dst_ref=dst.at[index_of], send_sem=send_sem.at[k],
            recv_sem=recv_sem.at[index_of], device_id=peer_of(t), device_id_type=MESH,
        )
        c.start()
        sends.append(c)
    return sends


def wait_all(src_ref, dst, peer_of, index_of, count, send_sem, recv_sem, sends):
    for k in range(1, count):
        src = lax.rem(index_of + count - k, count)
        pltpu.make_async_remote_copy(
            src_ref=src_ref(0), dst_ref=dst.at[src], send_sem=send_sem.at[k],
            recv_sem=recv_sem.at[src], device_id=peer_of(src), device_id_type=MESH,
        ).wait_recv()
    for c in sends:
        c.wait_send()


def weight_kernel(nf, scale, share_ref, gw_ref, chunks, recv1, redbuf, recv2, s1, r1, s2, r2):
    cols = chunks.shape[2]
    me_f = lax.axis_index("frame")
    me_s = lax.axis_index("space")
    peer = lambda t: (t, me_s)
    barrier = pltpu.get_barrier_semaphore()
    for k in range(1, nf):
        pl.semaphore_signal(
            barrier, inc=1, device_id=peer(lax.rem(me_f + k, nf)), device_id_type=MESH
        )
    for j in range(nf):
        chunks[j] = share_ref[:, j * cols:(j + 1) * cols]
    pl.semaphore_wait(barrier, nf - 1)
    first = lambda t: chunks.at[t]
    sends = exchange(first, recv1, peer, me_f, nf, s1, r1)
    recv1[me_f] = chunks[me_f]
    wait_all(first, recv1, peer, me_f, nf, s1, r1, sends)
    acc = recv1[0].astype(jnp.float32)
    for j in range(1, nf):
        acc = acc + recv1[j].astype(jnp.float32)
    acc = acc.astype(redbuf.dtype)
    redbuf[...] = acc
    recv2[me_f] = acc
    second = lambda t: redbuf
    sends = exchange(second, recv2, peer, me_f, nf, s2, r2)
    wait_all(second, recv2, peer, me_f, nf, s2, r2, sends)
    for j in range(nf):
        gw_ref[:, j * cols:(j + 1) * cols] = recv2[j].astype(jnp.float32) * scale


def sums_kernel(nf, ns, sums_ref, gm_ref, msum1, mbuf, msum2, s1, r1, s2, r2):
    me_f = lax.axis_index("frame")
    me_s = lax.axis_index("space")
    fpeer = lambda t: (t, me_s)
    speer = lambda t: (me_f, t)
    barrier_with(
        [fpeer(lax.rem(me_f + k, nf)) for k in range(1, nf)]
        + [speer(lax.rem(me_s + k, ns)) for k in range(1, ns)]
    )
    first = lambda t: sums_ref
    sends = exchange(first, msum1, fpeer, me_f, nf, s1, r1)
    msum1[me_f] = sums_ref[...]
    wait_all(first, msum1, fpeer, me_f, nf, s1, r1, sends)
    macc = msum1[0]
    for j in range(1, nf):
        macc = macc + msum1[j]
    mbuf[...] = macc
    msum2[me_s] = macc
    second = lambda t: mbuf
    sends = exchange(second, msum2, speer, me_s, ns, s2, r2)
    wait_all(second, msum2, speer, me_s, ns, s2, r2, sends)
    total = msum2[0]
    for j in range(1, ns):
        total = total + msum2[j]
    gm_ref[...] = total


def reduce_weight(share, nf, scale):
    rows, width = share.shape
    cols = width // nf
    vmem = pl.BlockSpec(memory_space=pltpu.VMEM)
    return pl.pallas_call(
        functools.partial(weight_kernel, nf, scale),
        out_shape=jax.ShapeDtypeStruct((rows, width), jnp.float32),
        in_specs=[vmem],
        out_specs=vmem,
        scratch_shapes=[
            pltpu.VMEM((nf, rows, cols), share.dtype),
            pltpu.VMEM((nf, rows, cols), share.dtype),
            pltpu.VMEM((rows, cols), share.dtype),
            pltpu.VMEM((nf, rows, cols), share.dtype),
        ]
        + [pltpu.SemaphoreType.DMA((nf,))] * 4,
        compiler_params=pltpu.CompilerParams(collective_id=0, has_side_effects=True),
    )(share)


def reduce_sums(sums, nf, ns):
    vmem = pl.BlockSpec(memory_space=pltpu.VMEM)
    return pl.pallas_call(
        functools.partial(sums_kernel, nf, ns),
        out_shape=jax.ShapeDtypeStruct(sums.shape, jnp.float32),
        in_specs=[vmem],
        out_specs=vmem,
        scratch_shapes=[
            pltpu.VMEM((nf,) + sums.shape, jnp.float32),
            pltpu.VMEM(sums.shape, jnp.float32),
            pltpu.VMEM((ns,) + sums.shape, jnp.float32),
        ]
        + [pltpu.SemaphoreType.DMA((nf,)), pltpu.SemaphoreType.DMA((nf,))]
        + [pltpu.SemaphoreType.DMA((ns,)), pltpu.SemaphoreType.DMA((ns,))],
        compiler_params=pltpu.CompilerParams(collective_id=1, has_side_effects=True),
    )(sums)


def per_device(
    hidden_in, attn_cotangent, w_qkv, modulation_table, snr_table, timestep, weight_index
):
    clip_count, frame_dev, row_dev, col_count, model_width = hidden_in.shape
    frame_n = lax.axis_size("frame")
    space_n = lax.axis_size("space")
    positions = row_dev * col_count
    w_full = lax.all_gather(w_qkv, "space", axis=0, tiled=True)
    both = jnp.stack(
        [
            hidden_in.reshape(clip_count, frame_dev, positions, model_width),
            attn_cotangent.reshape(clip_count, frame_dev, positions, model_width),
        ],
        axis=3,
    )
    both = lax.all_to_all(both, "frame", split_axis=2, concat_axis=1, tiled=True)
    frames = both.shape[1]
    across = both.shape[2]
    values_in = both[:, :, :, 0].astype(jnp.float32)
    average = jnp.mean(values_in, axis=-1, keepdims=True)
    centered = values_in - average
    variance = jnp.mean(centered * centered, axis=-1, keepdims=True)
    inverse_std = lax.rsqrt(variance + 1e-06)
    normed = centered * inverse_std
    modulation = modulation_table[timestep].astype(jnp.float32)
    shift = modulation[:, 0][:, None, None, :]
    scale = modulation[:, 1][:, None, None, :]
    modulated = (normed * (1.0 + scale) + shift).astype(jnp.bfloat16)
    mod_rows = modulated.reshape(-1, model_width)
    projected = jnp.dot(mod_rows, w_full, preferred_element_type=jnp.float32).astype(jnp.bfloat16)
    pieces = projected.reshape(clip_count, frames, across, 3, HEADS, HEAD_DIM)
    loss_weight = snr_table[weight_index]
    upstream = (
        loss_weight[:, None, None, None] * both[:, :, :, 1].astype(jnp.float32)
    ).astype(jnp.bfloat16)
    upstream = upstream.reshape(clip_count, frames, across, HEADS, HEAD_DIM)
    head_grads = attend_back(pieces[:, :, :, 0], pieces[:, :, :, 1], pieces[:, :, :, 2], upstream)
    grad_rows = jnp.stack(head_grads, axis=3).reshape(-1, 3 * model_width)
    grad_scale_factor = float(mod_rows.shape[0] * frame_n * space_n) ** (-0.5)
    term = lax.dot_general(
        mod_rows, grad_rows, (((0,), (0,)), ((), ())), preferred_element_type=jnp.float32
    ).astype(jnp.bfloat16)
    term, grad_rows = lax.optimization_barrier((term, grad_rows))
    col_blk = 3 * model_width // frame_n
    share = lax.psum_scatter(term, "space", scatter_dimension=0, tiled=True)
    grad_hidden = lax.dot_general(
        grad_rows, w_full, (((1,), (1,)), ((), ())), preferred_element_type=jnp.float32
    )
    grad_hidden = grad_hidden.reshape(values_in.shape)
    local_sums = jnp.stack(
        [jnp.sum(grad_hidden, axis=(1, 2)), jnp.sum(grad_hidden * normed, axis=(1, 2))],
        axis=1,
    )
    local_sums = local_sums.reshape(-1, model_width)
    gm = reduce_sums(local_sums, frame_n, space_n)
    grad_weight = reduce_weight(share, frame_n, grad_scale_factor)
    grad_modulation = gm.reshape(clip_count, 2, model_width) * grad_scale_factor
    grad_normed = grad_hidden * (1.0 + scale)
    grad_input = (
        grad_normed
        - jnp.mean(grad_normed, axis=-1, keepdims=True)
        - normed * jnp.mean(grad_normed * normed, axis=-1, keepdims=True)
    ) * inverse_std
    grad_input = grad_input.astype(jnp.bfloat16)
    grad_input = lax.all_to_all(grad_input, "frame", split_axis=1, concat_axis=2, tiled=True)
    grad_input = grad_input.reshape(clip_count, frame_dev, row_dev, col_count, model_width)
    return (grad_input, grad_weight, grad_modulation)


def solution(mesh):
    in_specs = (
        P(None, "frame", "space", None, None),
        P(None, "frame", "space", None, None),
        P("space", None),
        P(),
        P(),
        P(),
        P(),
    )
    out_specs = (P(None, "frame", "space", None, None), P("space", None), P())
    return jax.shard_map(
        per_device, mesh=mesh, in_specs=in_specs, out_specs=out_specs, check_vma=False
    )
```

```python
import functools

import jax
import jax.numpy as jnp
from jax import lax
from jax.experimental import pallas as pl
from jax.experimental.pallas import tpu as pltpu
from jax.sharding import PartitionSpec as P

MESH = pl.DeviceIdType.MESH

HEADS = 16
HEAD_DIM = 72


def attend_back(queries, keys, values, upstream):
    factor = queries.shape[-1] ** (-0.5)
    f32 = jnp.float32
    high = lax.Precision.HIGH
    scores = jnp.einsum("bfxhe,bgxhe->bxhfg", queries, keys, preferred_element_type=f32) * factor
    expd = jnp.exp(scores)
    probs = expd / jnp.sum(expd, axis=-1, keepdims=True)
    grad_probs = jnp.einsum("bfxhe,bgxhe->bxhfg", upstream, values, preferred_element_type=f32)
    grad_values = jnp.einsum(
        "bxhfg,bfxhe->bgxhe", probs, upstream.astype(f32), precision=high
    )
    grad_scores = probs * (grad_probs - jnp.sum(probs * grad_probs, axis=-1, keepdims=True))
    grad_queries = jnp.einsum(
        "bxhfg,bgxhe->bfxhe", grad_scores, keys.astype(f32), precision=high
    ) * factor
    grad_keys = jnp.einsum(
        "bxhfg,bfxhe->bgxhe", grad_scores, queries.astype(f32), precision=high
    ) * factor
    return (
        grad_queries.astype(jnp.bfloat16),
        grad_keys.astype(jnp.bfloat16),
        grad_values.astype(jnp.bfloat16),
    )


def barrier_with(peers):
    barrier = pltpu.get_barrier_semaphore()
    for p in peers:
        pl.semaphore_signal(barrier, inc=1, device_id=p, device_id_type=MESH)
    pl.semaphore_wait(barrier, len(peers))


def exchange(src_ref, dst, peer_of, index_of, count, send_sem, recv_sem):
    sends = []
    for k in range(1, count):
        t = lax.rem(index_of + k, count)
        c = pltpu.make_async_remote_copy(
            src_ref=src_ref(t), dst_ref=dst.at[index_of], send_sem=send_sem.at[k],
            recv_sem=recv_sem.at[index_of], device_id=peer_of(t), device_id_type=MESH,
        )
        c.start()
        sends.append(c)
    return sends


def wait_all(src_ref, dst, peer_of, index_of, count, send_sem, recv_sem, sends):
    for k in range(1, count):
        src = lax.rem(index_of + count - k, count)
        pltpu.make_async_remote_copy(
            src_ref=src_ref(0), dst_ref=dst.at[src], send_sem=send_sem.at[k],
            recv_sem=recv_sem.at[src], device_id=peer_of(src), device_id_type=MESH,
        ).wait_recv()
    for c in sends:
        c.wait_send()


def weight_kernel(nf, scale, share_ref, gw_ref, chunks, recv1, redbuf, recv2, s1, r1, s2, r2):
    cols = chunks.shape[2]
    me_f = lax.axis_index("frame")
    me_s = lax.axis_index("space")
    peer = lambda t: (t, me_s)
    barrier = pltpu.get_barrier_semaphore()
    for k in range(1, nf):
        pl.semaphore_signal(
            barrier, inc=1, device_id=peer(lax.rem(me_f + k, nf)), device_id_type=MESH
        )
    for j in range(nf):
        chunks[j] = share_ref[:, j * cols:(j + 1) * cols]
    pl.semaphore_wait(barrier, nf - 1)
    first = lambda t: chunks.at[t]
    sends = exchange(first, recv1, peer, me_f, nf, s1, r1)
    recv1[me_f] = chunks[me_f]
    wait_all(first, recv1, peer, me_f, nf, s1, r1, sends)
    acc = recv1[0].astype(jnp.float32)
    for j in range(1, nf):
        acc = acc + recv1[j].astype(jnp.float32)
    acc = acc.astype(redbuf.dtype)
    redbuf[...] = acc
    second = lambda t: redbuf
    sends = exchange(second, recv2, peer, me_f, nf, s2, r2)
    recv2[me_f] = acc
    wait_all(second, recv2, peer, me_f, nf, s2, r2, sends)
    for j in range(nf):
        gw_ref[:, j * cols:(j + 1) * cols] = recv2[j].astype(jnp.float32) * scale


def sums_kernel(nf, ns, sums_ref, gm_ref, msum1, mbuf, msum2, s1, r1, s2, r2):
    me_f = lax.axis_index("frame")
    me_s = lax.axis_index("space")
    fpeer = lambda t: (t, me_s)
    speer = lambda t: (me_f, t)
    barrier_with(
        [fpeer(lax.rem(me_f + k, nf)) for k in range(1, nf)]
        + [speer(lax.rem(me_s + k, ns)) for k in range(1, ns)]
    )
    first = lambda t: sums_ref
    sends = exchange(first, msum1, fpeer, me_f, nf, s1, r1)
    msum1[me_f] = sums_ref[...]
    wait_all(first, msum1, fpeer, me_f, nf, s1, r1, sends)
    macc = msum1[0]
    for j in range(1, nf):
        macc = macc + msum1[j]
    mbuf[...] = macc
    msum2[me_s] = macc
    second = lambda t: mbuf
    sends = exchange(second, msum2, speer, me_s, ns, s2, r2)
    wait_all(second, msum2, speer, me_s, ns, s2, r2, sends)
    total = msum2[0]
    for j in range(1, ns):
        total = total + msum2[j]
    gm_ref[...] = total


def reduce_weight(share, nf, scale):
    rows, width = share.shape
    cols = width // nf
    vmem = pl.BlockSpec(memory_space=pltpu.VMEM)
    return pl.pallas_call(
        functools.partial(weight_kernel, nf, scale),
        out_shape=jax.ShapeDtypeStruct((rows, width), jnp.float32),
        in_specs=[vmem],
        out_specs=vmem,
        scratch_shapes=[
            pltpu.VMEM((nf, rows, cols), share.dtype),
            pltpu.VMEM((nf, rows, cols), share.dtype),
            pltpu.VMEM((rows, cols), share.dtype),
            pltpu.VMEM((nf, rows, cols), share.dtype),
        ]
        + [pltpu.SemaphoreType.DMA((nf,))] * 4,
        compiler_params=pltpu.CompilerParams(collective_id=0, has_side_effects=True),
    )(share)


def reduce_sums(sums, nf, ns):
    vmem = pl.BlockSpec(memory_space=pltpu.VMEM)
    return pl.pallas_call(
        functools.partial(sums_kernel, nf, ns),
        out_shape=jax.ShapeDtypeStruct(sums.shape, jnp.float32),
        in_specs=[vmem],
        out_specs=vmem,
        scratch_shapes=[
            pltpu.VMEM((nf,) + sums.shape, jnp.float32),
            pltpu.VMEM(sums.shape, jnp.float32),
            pltpu.VMEM((ns,) + sums.shape, jnp.float32),
        ]
        + [pltpu.SemaphoreType.DMA((nf,)), pltpu.SemaphoreType.DMA((nf,))]
        + [pltpu.SemaphoreType.DMA((ns,)), pltpu.SemaphoreType.DMA((ns,))],
        compiler_params=pltpu.CompilerParams(collective_id=1, has_side_effects=True),
    )(sums)


def per_device(
    hidden_in, attn_cotangent, w_qkv, modulation_table, snr_table, timestep, weight_index
):
    clip_count, frame_dev, row_dev, col_count, model_width = hidden_in.shape
    frame_n = lax.axis_size("frame")
    space_n = lax.axis_size("space")
    positions = row_dev * col_count
    w_full = lax.all_gather(w_qkv, "space", axis=0, tiled=True)
    both = jnp.stack(
        [
            hidden_in.reshape(clip_count, frame_dev, positions, model_width),
            attn_cotangent.reshape(clip_count, frame_dev, positions, model_width),
        ],
        axis=3,
    )
    both = lax.all_to_all(both, "frame", split_axis=2, concat_axis=1, tiled=True)
    frames = both.shape[1]
    across = both.shape[2]
    values_in = both[:, :, :, 0].astype(jnp.float32)
    average = jnp.mean(values_in, axis=-1, keepdims=True)
    centered = values_in - average
    variance = jnp.mean(centered * centered, axis=-1, keepdims=True)
    inverse_std = lax.rsqrt(variance + 1e-06)
    normed = centered * inverse_std
    modulation = modulation_table[timestep].astype(jnp.float32)
    shift = modulation[:, 0][:, None, None, :]
    scale = modulation[:, 1][:, None, None, :]
    modulated = (normed * (1.0 + scale) + shift).astype(jnp.bfloat16)
    mod_rows = modulated.reshape(-1, model_width)
    projected = jnp.dot(mod_rows, w_full, preferred_element_type=jnp.float32).astype(jnp.bfloat16)
    pieces = projected.reshape(clip_count, frames, across, 3, HEADS, HEAD_DIM)
    loss_weight = snr_table[weight_index]
    upstream = (
        loss_weight[:, None, None, None] * both[:, :, :, 1].astype(jnp.float32)
    ).astype(jnp.bfloat16)
    upstream = upstream.reshape(clip_count, frames, across, HEADS, HEAD_DIM)
    head_grads = attend_back(pieces[:, :, :, 0], pieces[:, :, :, 1], pieces[:, :, :, 2], upstream)
    grad_rows = jnp.stack(head_grads, axis=3).reshape(-1, 3 * model_width)
    grad_scale_factor = float(mod_rows.shape[0] * frame_n * space_n) ** (-0.5)
    term = lax.dot_general(
        mod_rows, grad_rows, (((0,), (0,)), ((), ())), preferred_element_type=jnp.float32
    ).astype(jnp.bfloat16)
    term, grad_rows = lax.optimization_barrier((term, grad_rows))
    col_blk = 3 * model_width // frame_n
    share = lax.psum_scatter(term, "space", scatter_dimension=0, tiled=True)
    grad_hidden = lax.dot_general(
        grad_rows, w_full, (((1,), (1,)), ((), ())), preferred_element_type=jnp.float32
    )
    grad_hidden = grad_hidden.reshape(values_in.shape)
    local_sums = jnp.stack(
        [jnp.sum(grad_hidden, axis=(1, 2)), jnp.sum(grad_hidden * normed, axis=(1, 2))],
        axis=1,
    )
    local_sums = local_sums.reshape(-1, model_width)
    gm = reduce_sums(local_sums, frame_n, space_n)
    grad_weight = reduce_weight(share, frame_n, grad_scale_factor)
    grad_modulation = gm.reshape(clip_count, 2, model_width) * grad_scale_factor
    grad_normed = grad_hidden * (1.0 + scale)
    grad_input = (
        grad_normed
        - jnp.mean(grad_normed, axis=-1, keepdims=True)
        - normed * jnp.mean(grad_normed * normed, axis=-1, keepdims=True)
    ) * inverse_std
    grad_input = grad_input.astype(jnp.bfloat16)
    grad_input = lax.all_to_all(grad_input, "frame", split_axis=1, concat_axis=2, tiled=True)
    grad_input = grad_input.reshape(clip_count, frame_dev, row_dev, col_count, model_width)
    return (grad_input, grad_weight, grad_modulation)


def solution(mesh):
    in_specs = (
        P(None, "frame", "space", None, None),
        P(None, "frame", "space", None, None),
        P("space", None),
        P(),
        P(),
        P(),
        P(),
    )
    out_specs = (P(None, "frame", "space", None, None), P("space", None), P())
    return jax.shard_map(
        per_device, mesh=mesh, in_specs=in_specs, out_specs=out_specs, check_vma=False
    )
```
